256 devices in a mesh: seq: 128 (over x_hi, z, y, core), chan: 2 (over x_lo).
Axes of the slice: x: 4 (x_hi: 2, x_lo: 2; x = x_hi * 2 + x_lo), y: 4, z: 8, core: 2. Of those that a mesh axis runs over, the one named last changes fastest.
Arguments:
- projected: bfloat16 [16384, 3, 2048], P('seq', None, 'chan'), may hold values from -6 to 6
- skip_gain: float32 [2048], P('chan'), may hold values from 0.5 to 1.5
- out_weight: bfloat16 [2048, 4096], P('chan'), may hold values from -0.125 to 0.125
- long_filter: float32 [16384, 2048], P('seq', 'chan'), may hold values from -0.125 to 0.125
- cotangent: bfloat16 [16384, 4096], P('seq', 'chan'), may hold values from -6 to 6
Outputs:
- mixed: bfloat16 [16384, 4096], P('seq', 'chan')
- grad_projected: bfloat16 [16384, 3, 2048], P('seq', None, 'chan')
- grad_filter: float32 [16384, 2048], P('seq', 'chan')
The draws below stay inside these ranges and needn't reach their ends.
All inputs are finite; a program needn't handle non-finite values.
Results may differ from the reference program's by a relative error of at most 0.0049.
Values may be sent and summed in bfloat16 or wider, within the bound.
No kernel may reach another device: no remote copies, remote signals or barrier semaphores. Data moves between devices by JAX's collectives and lax.ppermute only.
A program may use at most 128 MiB of HBM per device.

```python
import jax
import jax.numpy as jnp

D = 4096
C = 2048
TOKENS = 16384


def steps_of(key, extent, pieces, least, largest):
    level = 1.0
    for dim, blocks in pieces:
        heights = jax.random.uniform(jax.random.fold_in(jax.random.fold_in(key, 6), dim), (blocks,), jnp.float32, least / len(pieces), largest / len(pieces))
        level = level * jnp.repeat(jnp.exp(heights), extent[dim] // blocks).reshape((-1,) + (1,) * (len(extent) - 1 - dim))
    return level


def normal_values(key, extent, spread, most, split=(), kind=jnp.bfloat16):
    gain = steps_of(key, extent, split, -0.22, 0.18) if split else 1.0
    entries = jax.random.normal(key, extent, jnp.float32) * spread * gain
    return jnp.minimum(jnp.maximum(entries, -most), most).astype(kind)


def setup_inputs(seed: int = 0) -> dict:
    streams_of = jax.random.split(jax.random.key(seed), 6)
    return {
        "projected": normal_values(streams_of[0], (TOKENS, 3, C), 1.0, 6.0, ((0, 128), (2, 2))),
        "skip_gain": jnp.clip(0.5 + 1.0 * jax.random.uniform(streams_of[1], (C,), jnp.float32) ** steps_of(streams_of[1], (C,), ((0, 2),), -0.2, 0.2), 0.5, 1.5),
        "out_weight": normal_values(streams_of[2], (C, D), C ** -0.5, 0.125, ((0, 2),)),
        "long_filter": normal_values(streams_of[3], (TOKENS, C), (TOKENS ** -0.5), 0.125, ((0, 128), (1, 2)), jnp.float32),
        "cotangent": normal_values(streams_of[4], (TOKENS, D), 1.0, 6.0, ((0, 128), (1, 2))),
    }


def reference(projected, skip_gain, out_weight, long_filter, cotangent):
    query = projected[:, 0].astype(jnp.float32)
    key_part = projected[:, 1].astype(jnp.float32)
    value_part = projected[:, 2].astype(jnp.float32)
    source = key_part * value_part
    span = 2 * TOKENS
    source_hat = jnp.fft.rfft(source, n=span, axis=0)
    filter_hat = jnp.fft.rfft(long_filter, n=span, axis=0)
    conv = jnp.fft.irfft(source_hat * filter_hat, n=span, axis=0)[:TOKENS]
    mixing = conv + skip_gain * source
    gated = (query * mixing).astype(jnp.bfloat16)
    mixed = jnp.dot(gated, out_weight, preferred_element_type=jnp.float32).astype(jnp.bfloat16)
    grad_gated = jnp.dot(cotangent, out_weight.T, preferred_element_type=jnp.float32)
    grad_query = (grad_gated * mixing).astype(jnp.bfloat16)
    grad_mixing = grad_gated * query
    grad_hat = jnp.fft.rfft(grad_mixing, n=span, axis=0)
    grad_source = jnp.fft.irfft(jnp.conj(filter_hat) * grad_hat, n=span, axis=0)[:TOKENS] + skip_gain * grad_mixing
    grad_filter = jnp.fft.irfft(jnp.conj(source_hat) * grad_hat, n=span, axis=0)[:TOKENS] * (TOKENS ** -0.5)
    grad_projected = jnp.stack([grad_query, (grad_source * value_part).astype(jnp.bfloat16), (grad_source * key_part).astype(jnp.bfloat16)], axis=1)
    return mixed, grad_projected, grad_filter
```

```python
import math

import jax
import jax.numpy as jnp
import numpy as np
from jax import lax
from jax.experimental import pallas as pl
from jax.experimental.pallas import tpu as pltpu
from jax.sharding import PartitionSpec as P

F32 = jnp.float32
BF16 = jnp.bfloat16
VMEM_LIMIT = 56 * 1024 * 1024


def params():
    return pltpu.CompilerParams(vmem_limit_bytes=VMEM_LIMIT)


def halves(table):
    high = table.astype(BF16)
    low = (table - high.astype(np.float64)).astype(BF16)
    return high, low


def tables(blocks, rows):
    length = 2 * blocks * rows
    k1 = np.arange(blocks)[:, None] + 0.5
    angle = 2.0 * np.pi * k1 * np.arange(blocks)[None, :] / (2 * blocks)
    outer = np.concatenate([np.cos(angle), -np.sin(angle)], axis=0)
    outer_high, outer_low = halves(outer)
    outer_both = np.concatenate([outer_high, outer_low], axis=1)
    back_high, back_low = halves(outer.T)
    turn = 2.0 * np.pi * k1 * np.arange(rows)[None, :] / length
    turn_re = np.cos(turn).astype(np.float32)
    turn_im = -np.sin(turn).astype(np.float32)
    grid = 2.0 * np.pi * (np.outer(np.arange(rows), np.arange(rows)) % rows) / rows
    cos, sin = np.cos(grid), np.sin(grid)
    inner_high, inner_low = halves(np.block([[cos, -sin], [sin, cos]]))
    return [outer_both, back_high, back_low, turn_re, turn_im, inner_high, inner_low]


def dot(a, b):
    return jnp.dot(a, b, preferred_element_type=F32)


def dot_t(a, b):
    return lax.dot_general(a, b, (((1,), (1,)), ((), ())), preferred_element_type=F32)


def split(x):
    high = x.astype(BF16)
    return high, (x - high.astype(F32)).astype(BF16)


def forward(signal_ref, first, stride, blocks, count, tabs, high_ref, low_ref, spec_ref):
    outer, _, _, turn_re, turn_im, inner_high, inner_low = tabs
    rows = signal_ref.shape[1]
    tre, tim = turn_re[...], turn_im[...]
    for pair in range(count // 2):
        x = jnp.concatenate(
            [
                signal_ref[pl.ds(first + 2 * pair + j, blocks, stride=stride), :].astype(BF16)
                for j in range(2)
            ],
            axis=1,
        )
        a = dot(outer[...], jnp.concatenate([x, x], axis=0))
        for j in range(2):
            are = a[:blocks, j * rows : (j + 1) * rows]
            aim = a[blocks:, j * rows : (j + 1) * rows]
            b = jnp.concatenate([are * tre - aim * tim, are * tim + aim * tre], axis=1)
            high, low = split(b)
            at = (2 * pair + j) * blocks
            high_ref[at : at + blocks, :] = high
            low_ref[at : at + blocks, :] = low
    spec_ref[...] = (
        dot(high_ref[...], inner_high[...])
        + dot(low_ref[...], inner_high[...])
        + dot(high_ref[...], inner_low[...])
    )


def inverse(high_ref, low_ref, part_ref, tabs, scale, blocks, count, out_ref, first, stride):
    _, back_high, back_low, turn_re, turn_im, inner_high, inner_low = tabs
    rows = out_ref.shape[1]
    tre, tim = turn_re[...] * scale, turn_im[...] * scale
    part_ref[...] = (
        dot_t(high_ref[...], inner_high[...])
        + dot_t(low_ref[...], inner_high[...])
        + dot_t(high_ref[...], inner_low[...])
    )
    for pair in range(count // 2):
        both = []
        for j in range(2):
            at = (2 * pair + j) * blocks
            cre = part_ref[at : at + blocks, :rows]
            cim = part_ref[at : at + blocks, rows:]
            both.append(jnp.concatenate([cre * tre + cim * tim, cim * tre - cre * tim], axis=0))
        high, low = split(jnp.concatenate(both, axis=1))
        y = dot(back_high[...], high) + dot(back_high[...], low) + dot(back_low[...], high)
        for j in range(2):
            out_ref[pl.ds(first + 2 * pair + j, blocks, stride=stride), :] = y[
                :, j * rows : (j + 1) * rows
            ]


def product(a_ref, b_ref, conj, high_ref, low_ref):
    half = a_ref.shape[1] // 2
    total = a_ref.shape[0]
    step = total // 8
    for i in range(8):
        at = slice(i * step, (i + 1) * step)
        ar, ai = a_ref[at, :half], a_ref[at, half:]
        br, bi = b_ref[at, :half], b_ref[at, half:]
        if conj:
            z = jnp.concatenate([ar * br + ai * bi, ar * bi - ai * br], axis=1)
        else:
            z = jnp.concatenate([ar * br - ai * bi, ar * bi + ai * br], axis=1)
        high, low = split(z)
        high_ref[at, :] = high
        low_ref[at, :] = low


def prep_kernel(proj_ref, filter_ref, out_ref):
    step, each, rows = out_ref.shape
    each //= 2
    source = proj_ref[1].astype(F32) * proj_ref[2].astype(F32)
    out_ref[:, :each, :] = source.T.reshape(step, each, rows).astype(BF16)
    out_ref[:, each:, :] = filter_ref[...].T.reshape(step, each, rows).astype(BF16)


def grad_kernel(
    chan_ref, w_ref, own_ref, other_ref, proj_ref, skip_ref, gm_ref, gg_ref, q_ref, ss_ref, sg_ref
):
    half = own_ref.shape[1]
    first = chan_ref[0] == 0
    own, other = own_ref[...], other_ref[...]
    low = jnp.where(first, own, other)
    high = jnp.where(first, other, own)
    gg = dot_t(w_ref[:, :half], low) + dot_t(w_ref[:, half:], high)
    query = proj_ref[0].astype(F32).T
    gm = gg * query
    skip = skip_ref[...]
    gg_ref[...] = gg
    q_ref[...] = query
    gm_ref[...] = gm.astype(BF16)
    sg_ref[...] = gm.T * skip
    ss_ref[...] = (proj_ref[1].astype(F32) * proj_ref[2].astype(F32) * skip).T


def conv_kernel(*refs):
    in_ref, gm_ref = refs[:2]
    tabs = refs[2:9]
    spec_ref, out_ref = refs[9:11]
    wide_ref, high_ref, low_ref, part_ref, back_ref = refs[11:]
    blocks, two, rows = in_ref.shape
    count = two // 2
    wide_ref[...] = in_ref[...].astype(F32).reshape(blocks * two, rows)
    for s in range(2):
        forward(
            wide_ref, s * count, two, blocks, count, tabs, high_ref, low_ref, spec_ref.at[s]
        )
    product(spec_ref.at[0], spec_ref.at[1], False, high_ref, low_ref)
    inverse(
        high_ref, low_ref, part_ref, tabs, 1.0 / (blocks * rows), blocks, count, back_ref, 0, count
    )
    out_ref[:, :count, :] = gm_ref[...]
    out_ref[:, count:, :] = back_ref[...].reshape(blocks, count, rows).astype(BF16)


def corr_kernel(*refs):
    in_ref, spec_ref = refs[:2]
    tabs = refs[2:9]
    out_ref = refs[9]
    wide_ref, high_ref, low_ref, part_ref, grad_ref, back_ref = refs[10:]
    blocks, count, rows = in_ref.shape
    wide_ref[...] = in_ref[...].astype(F32).reshape(blocks * count, rows)
    forward(wide_ref, 0, count, blocks, count, tabs, high_ref, low_ref, grad_ref)
    scale = 1.0 / (blocks * rows)
    for s, factor in ((1, scale), (0, scale / math.sqrt(blocks * rows))):
        product(spec_ref.at[s], grad_ref, True, high_ref, low_ref)
        inverse(
            high_ref, low_ref, part_ref, tabs, factor, blocks, count, back_ref, (1 - s) * count,
            2 * count,
        )
    out_ref[...] = back_ref[...].reshape(blocks, 2 * count, rows).astype(BF16)


def mix_kernel(
    chan_ref, conv_ref, ss_ref, q_ref, gg_ref, w_ref, send_ref, gated_ref, gq_ref
):
    @pl.when(pl.program_id(0) == 0)
    def _():
        mixing = conv_ref[...].astype(F32).reshape(ss_ref.shape) + ss_ref[...]
        gated_ref[...] = (mixing * q_ref[...]).T.astype(BF16)
        gq_ref[...] = (mixing * gg_ref[...]).T.astype(BF16)

    send_ref[...] = dot(gated_ref[...], w_ref[...]).astype(BF16)


def own_kernel(chan_ref, gated_ref, w_ref, out_ref):
    out_ref[...] = dot(gated_ref[...], w_ref[...])


def end_kernel(in_ref, sg_ref, gq_ref, proj_ref, gp_ref, gf_ref):
    step, two, rows = in_ref.shape
    count = two // 2
    gs = in_ref[:, :count, :].astype(F32).reshape(step * count, rows).T + sg_ref[...]
    gp_ref[0] = gq_ref[...]
    gp_ref[1] = (gs * proj_ref[2].astype(F32)).astype(BF16)
    gp_ref[2] = (gs * proj_ref[1].astype(F32)).astype(BF16)
    gf_ref[...] = in_ref[:, count:, :].astype(F32).reshape(step * count, rows).T


def local(projected, skip_gain, out_weight, long_filter, cotangent):
    blocks = lax.axis_size("seq")
    rows, channels = long_filter.shape
    each = channels // blocks
    width = out_weight.shape[1]
    half = width // 2
    chan = lax.axis_index("chan").astype(jnp.int32).reshape(1)
    proj = projected.transpose(1, 0, 2)
    skip = skip_gain.reshape(1, channels)
    tabs = [jnp.asarray(t) for t in tables(blocks, rows)]
    full = lambda shape: pl.BlockSpec(shape, lambda *_: (0,) * len(shape))
    tab_specs = [full(t.shape) for t in tabs]
    shape = jax.ShapeDtypeStruct

    other = lax.ppermute(cotangent, "chan", [(0, 1), (1, 0)])

    def exchange(x):
        return lax.all_to_all(x, "seq", 0, 0, tiled=True)

    parts = 4
    cb = channels // parts
    pb = blocks // parts
    signals = pl.pallas_call(
        prep_kernel,
        grid=(parts,),
        in_specs=[
            pl.BlockSpec((3, rows, cb), lambda i: (0, 0, i)),
            pl.BlockSpec((rows, cb), lambda i: (0, i)),
        ],
        out_specs=pl.BlockSpec((pb, 2 * each, rows), lambda i: (i, 0, 0)),
        out_shape=shape((blocks, 2 * each, rows), BF16),
        compiler_params=params(),
        name="prep",
    )(proj, long_filter)
    arrived = exchange(signals)

    gm, gg, query, skip_source, skip_grad = pl.pallas_call(
        grad_kernel,
        grid_spec=pltpu.PrefetchScalarGridSpec(
            num_scalar_prefetch=1,
            grid=(parts,),
            in_specs=[
                pl.BlockSpec((cb, width), lambda i, c: (i, 0)),
                full((rows, half)),
                full((rows, half)),
                pl.BlockSpec((3, rows, cb), lambda i, c: (0, 0, i)),
                pl.BlockSpec((1, cb), lambda i, c: (0, i)),
            ],
            out_specs=[pl.BlockSpec((cb, rows), lambda i, c: (i, 0))] * 4
            + [pl.BlockSpec((rows, cb), lambda i, c: (0, i))],
        ),
        out_shape=[shape((channels, rows), BF16)]
        + [shape((channels, rows), F32)] * 3
        + [shape((rows, channels), F32)],
        compiler_params=params(),
        name="grad",
    )(chan, out_weight, cotangent, other, proj, skip)

    spec_shape = (each * blocks, 2 * rows)
    spectra, mid = pl.pallas_call(
        conv_kernel,
        out_shape=[shape((2,) + spec_shape, F32), shape((blocks, 2 * each, rows), BF16)],
        scratch_shapes=[
            pltpu.VMEM((blocks * 2 * each, rows), F32),
            pltpu.VMEM(spec_shape, BF16),
            pltpu.VMEM(spec_shape, BF16),
            pltpu.VMEM(spec_shape, F32),
            pltpu.VMEM((blocks * each, rows), F32),
        ],
        compiler_params=params(),
        name="conv",
    )(arrived, gm.reshape(blocks, each, rows), *tabs)
    back = exchange(mid)

    pair = pl.pallas_call(
        corr_kernel,
        grid=(1,),
        in_specs=[full((blocks, each, rows)), full((2,) + spec_shape)] + tab_specs,
        out_specs=full((blocks, 2 * each, rows)),
        out_shape=shape((blocks, 2 * each, rows), BF16),
        scratch_shapes=[
            pltpu.VMEM((blocks * each, rows), F32),
            pltpu.VMEM(spec_shape, BF16),
            pltpu.VMEM(spec_shape, BF16),
            pltpu.VMEM(spec_shape, F32),
            pltpu.VMEM(spec_shape, F32),
            pltpu.VMEM((blocks * 2 * each, rows), F32),
        ],
        compiler_params=params(),
        name="corr",
    )(back, spectra, *tabs)
    last = exchange(pair)

    wb = half // 4
    send, gated, grad_query = pl.pallas_call(
        mix_kernel,
        grid_spec=pltpu.PrefetchScalarGridSpec(
            num_scalar_prefetch=1,
            grid=(4,),
            in_specs=[
                pl.BlockSpec((blocks, each, rows), lambda i, c: (0, 1, 0)),
                full((channels, rows)),
                full((channels, rows)),
                full((channels, rows)),
                pl.BlockSpec((channels, wb), lambda i, c: (0, (1 - c[0]) * 4 + i)),
            ],
            out_specs=[
                pl.BlockSpec((rows, wb), lambda i, c: (0, i)),
                full((rows, channels)),
                full((rows, channels)),
            ],
        ),
        out_shape=[
            shape((rows, half), BF16),
            shape((rows, channels), BF16),
            shape((rows, channels), BF16),
        ],
        compiler_params=params(),
        name="mix",
    )(chan, back, skip_source, query, gg, out_weight)
    received = lax.ppermute(send, "chan", [(0, 1), (1, 0)])
    kept = pl.pallas_call(
        own_kernel,
        grid_spec=pltpu.PrefetchScalarGridSpec(
            num_scalar_prefetch=1,
            grid=(4,),
            in_specs=[
                full((rows, channels)),
                pl.BlockSpec((channels, wb), lambda i, c: (0, c[0] * 4 + i)),
            ],
            out_specs=pl.BlockSpec((rows, wb), lambda i, c: (0, i)),
        ),
        out_shape=shape((rows, half), F32),
        compiler_params=params(),
        name="own",
    )(chan, gated, out_weight)
    mixed = (kept + received.astype(F32)).astype(BF16)

    grad_projected, grad_filter = pl.pallas_call(
        end_kernel,
        grid=(parts,),
        in_specs=[
            pl.BlockSpec((pb, 2 * each, rows), lambda i: (i, 0, 0)),
            pl.BlockSpec((rows, cb), lambda i: (0, i)),
            pl.BlockSpec((rows, cb), lambda i: (0, i)),
            pl.BlockSpec((3, rows, cb), lambda i: (0, 0, i)),
        ],
        out_specs=[
            pl.BlockSpec((3, rows, cb), lambda i: (0, 0, i)),
            pl.BlockSpec((rows, cb), lambda i: (0, i)),
        ],
        out_shape=[shape((3, rows, channels), BF16), shape((rows, channels), F32)],
        compiler_params=params(),
        name="end",
    )(last, skip_grad, grad_query, proj)
    return mixed, grad_projected.transpose(1, 0, 2), grad_filter


def solution(mesh):
    in_specs = (
        P("seq", None, "chan"),
        P("chan"),
        P("chan", None),
        P("seq", "chan"),
        P("seq", "chan"),
    )
    out_specs = (P("seq", "chan"), P("seq", None, "chan"), P("seq", "chan"))
    return jax.shard_map(local, mesh=mesh, in_specs=in_specs, out_specs=out_specs, check_vma=False)
```

```python
import math

import jax
import jax.numpy as jnp
import numpy as np
from jax import lax
from jax.experimental import pallas as pl
from jax.experimental.pallas import tpu as pltpu
from jax.sharding import PartitionSpec as P

F32 = jnp.float32
BF16 = jnp.bfloat16
VMEM_LIMIT = 20 * 1024 * 1024


def params():
    return pltpu.CompilerParams(vmem_limit_bytes=VMEM_LIMIT)


def halves(table):
    high = table.astype(BF16)
    low = (table - high.astype(np.float64)).astype(BF16)
    return high, low


def tables(blocks, rows):
    length = 2 * blocks * rows
    k1 = np.arange(blocks)[:, None] + 0.5
    angle = 2.0 * np.pi * k1 * np.arange(blocks)[None, :] / (2 * blocks)
    outer = np.concatenate([np.cos(angle), -np.sin(angle)], axis=0)
    outer_high, outer_low = halves(outer)
    outer_both = np.concatenate([outer_high, outer_low], axis=1)
    back_high, back_low = halves(outer.T)
    turn = 2.0 * np.pi * k1 * np.arange(rows)[None, :] / length
    turn_re = np.cos(turn).astype(np.float32)
    turn_im = -np.sin(turn).astype(np.float32)
    grid = 2.0 * np.pi * (np.outer(np.arange(rows), np.arange(rows)) % rows) / rows
    cos, sin = np.cos(grid), np.sin(grid)
    inner = np.block([[cos, -sin], [sin, cos]])
    return [outer_both, back_high, back_low, turn_re, turn_im, *halves(inner), *halves(inner.T)]


def dot(a, b):
    return jnp.dot(a, b, preferred_element_type=F32)


def transform(high_ref, low_ref, table_high, table_low):
    return (
        dot(high_ref[...], table_high[...])
        + dot(low_ref[...], table_high[...])
        + dot(high_ref[...], table_low[...])
    )


def dot_t(a, b):
    return lax.dot_general(a, b, (((1,), (1,)), ((), ())), preferred_element_type=F32)


def split(x):
    high = x.astype(BF16)
    return high, (x - high.astype(F32)).astype(BF16)


def forward(signal_ref, first, stride, blocks, count, tabs, high_ref, low_ref, spec_ref):
    outer, _, _, turn_re, turn_im, inner_high, inner_low, _, _ = tabs
    rows = signal_ref.shape[1]
    tre, tim = turn_re[...], turn_im[...]
    for pair in range(count // 2):
        x = jnp.concatenate(
            [
                signal_ref[pl.ds(first + 2 * pair + j, blocks, stride=stride), :].astype(BF16)
                for j in range(2)
            ],
            axis=1,
        )
        a = dot(outer[...], jnp.concatenate([x, x], axis=0))
        for j in range(2):
            are = a[:blocks, j * rows : (j + 1) * rows]
            aim = a[blocks:, j * rows : (j + 1) * rows]
            b = jnp.concatenate([are * tre - aim * tim, are * tim + aim * tre], axis=1)
            high, low = split(b)
            at = (2 * pair + j) * blocks
            high_ref[at : at + blocks, :] = high
            low_ref[at : at + blocks, :] = low
    spec_ref[...] = transform(high_ref, low_ref, inner_high, inner_low)


def inverse(high_ref, low_ref, part_ref, tabs, scale, blocks, count, out_ref, first, stride):
    _, back_high, back_low, turn_re, turn_im, _, _, inner_high, inner_low = tabs
    rows = out_ref.shape[1]
    tre, tim = turn_re[...] * scale, turn_im[...] * scale
    part_ref[...] = transform(high_ref, low_ref, inner_high, inner_low)
    for pair in range(count // 2):
        both = []
        for j in range(2):
            at = (2 * pair + j) * blocks
            cre = part_ref[at : at + blocks, :rows]
            cim = part_ref[at : at + blocks, rows:]
            both.append(jnp.concatenate([cre * tre + cim * tim, cim * tre - cre * tim], axis=0))
        high, low = split(jnp.concatenate(both, axis=1))
        y = dot(back_high[...], high) + dot(back_high[...], low) + dot(back_low[...], high)
        for j in range(2):
            out_ref[pl.ds(first + 2 * pair + j, blocks, stride=stride), :] = y[
                :, j * rows : (j + 1) * rows
            ]


def product(a_ref, b_ref, conj, high_ref, low_ref):
    half = a_ref.shape[1] // 2
    total = a_ref.shape[0]
    step = total // 8
    for i in range(8):
        at = slice(i * step, (i + 1) * step)
        ar, ai = a_ref[at, :half], a_ref[at, half:]
        br, bi = b_ref[at, :half], b_ref[at, half:]
        if conj:
            z = jnp.concatenate([ar * br + ai * bi, ar * bi - ai * br], axis=1)
        else:
            z = jnp.concatenate([ar * br - ai * bi, ar * bi + ai * br], axis=1)
        high, low = split(z)
        high_ref[at, :] = high
        low_ref[at, :] = low


def prep_kernel(proj_hbm, filter_hbm, out_hbm, pair_ref, filter_ref, out_ref, in_sem, out_sem):
    parts, _, rows, width = pair_ref.shape
    step, each = out_ref.shape[1], out_ref.shape[2] // 2
    reads, writes = [], []
    for i in range(parts):
        at = slice(i * width, (i + 1) * width)
        reads.append(
            (
                pltpu.make_async_copy(proj_hbm.at[1:3, :, at], pair_ref.at[i], in_sem.at[i, 0]),
                pltpu.make_async_copy(filter_hbm.at[:, at], filter_ref.at[i], in_sem.at[i, 1]),
            )
        )
        writes.append(
            pltpu.make_async_copy(
                out_ref.at[i], out_hbm.at[i * step : (i + 1) * step], out_sem.at[i]
            )
        )
    for pair, taps in reads:
        pair.start()
        taps.start()
    for i in range(parts):
        pair, taps = reads[i]
        pair.wait()
        source = pair_ref[i, 0].astype(F32) * pair_ref[i, 1].astype(F32)
        out_ref[i, :, :each, :] = source.T.reshape(step, each, rows).astype(BF16)
        taps.wait()
        out_ref[i, :, each:, :] = filter_ref[i].T.reshape(step, each, rows).astype(BF16)
        writes[i].start()
    for write in writes:
        write.wait()


def grad_kernel(
    chan_ref, w_ref, own_ref, other_ref, proj_ref, skip_ref, gm_ref, q_ref, gg_ref, ss_ref,
    sg_ref,
):
    half = own_ref.shape[1]
    first = chan_ref[0] == 0
    own, other = own_ref[...], other_ref[...]
    low = jnp.where(first, own, other)
    high = jnp.where(first, other, own)
    gg = dot_t(w_ref[:, :half], low) + dot_t(w_ref[:, half:], high)
    query = proj_ref[0].astype(F32).T
    gm = gg * query
    skip = skip_ref[...]
    gg_ref[...] = gg
    q_ref[...] = query.astype(BF16)
    gm_ref[...] = gm.astype(BF16)
    sg_ref[...] = gm.T * skip
    ss_ref[...] = (proj_ref[1].astype(F32) * proj_ref[2].astype(F32) * skip).T


def conv_kernel(*refs):
    in_ref, gm_hbm = refs[:2]
    tabs = refs[2:11]
    spec_ref, out_ref = refs[11:13]
    wide_ref, high_ref, low_ref, part_ref, back_ref, gm_sem = refs[13:]
    blocks, two, rows = in_ref.shape
    count = two // 2
    gm_copy = pltpu.make_async_copy(gm_hbm, out_ref.at[:, :count, :], gm_sem)
    gm_copy.start()
    wide_ref[...] = in_ref[...].astype(F32).reshape(blocks * two, rows)
    for s in range(2):
        forward(
            wide_ref, s * count, two, blocks, count, tabs, high_ref, low_ref, spec_ref.at[s]
        )
    product(spec_ref.at[0], spec_ref.at[1], False, high_ref, low_ref)
    inverse(
        high_ref, low_ref, part_ref, tabs, 1.0 / (blocks * rows), blocks, count, back_ref, 0, count
    )
    gm_copy.wait()
    out_ref[:, count:, :] = back_ref[...].reshape(blocks, count, rows).astype(BF16)


def corr_kernel(*refs):
    in_ref, spec_ref = refs[:2]
    tabs = refs[2:11]
    out_ref = refs[11]
    wide_ref, high_ref, low_ref, part_ref, grad_ref, back_ref = refs[12:]
    blocks, two, rows = out_ref.shape
    count = two // 2
    wide_ref[...] = in_ref[:, :count, :].astype(F32).reshape(blocks * count, rows)
    forward(wide_ref, 0, count, blocks, count, tabs, high_ref, low_ref, grad_ref)
    scale = 1.0 / (blocks * rows)
    for s, factor in ((1, scale), (0, scale / math.sqrt(blocks * rows))):
        product(spec_ref.at[s], grad_ref, True, high_ref, low_ref)
        inverse(
            high_ref, low_ref, part_ref, tabs, factor, blocks, count, back_ref, (1 - s) * count, two
        )
    out_ref[...] = back_ref[...].reshape(blocks, two, rows).astype(BF16)


def weight_copies(w_hbm, chan, buf_ref, sem_ref):
    parts, _, width = buf_ref.shape
    return [
        pltpu.make_async_copy(
            w_hbm.at[:, pl.ds(pl.multiple_of((chan * parts + i) * width, width), width)],
            buf_ref.at[i],
            sem_ref.at[i],
        )
        for i in range(parts)
    ]


def mix_kernel(
    chan_ref, in_ref, ss_ref, q_ref, w_hbm, send_hbm, gated_ref, buf_ref, send_ref, in_sem, out_sem
):
    parts, _, width = buf_ref.shape
    copies = weight_copies(w_hbm, 1 - chan_ref[0], buf_ref, in_sem)
    for copy in copies:
        copy.start()
    count = in_ref.shape[1] // 2
    mixing = in_ref[:, count:, :].astype(F32).reshape(ss_ref.shape) + ss_ref[...]
    gated_ref[...] = (mixing * q_ref[...].astype(F32)).T.astype(BF16)
    writes = []
    for i, copy in enumerate(copies):
        copy.wait()
        send_ref[i] = dot(gated_ref[...], buf_ref[i]).astype(BF16)
        write = pltpu.make_async_copy(
            send_ref.at[i], send_hbm.at[:, i * width : (i + 1) * width], out_sem.at[i]
        )
        write.start()
        writes.append(write)
    for write in writes:
        write.wait()


def own_kernel(
    chan_ref, in_ref, ss_ref, gg_ref, gated_ref, w_hbm, out_ref, gp_hbm, buf_ref, gq_ref, in_sem, out_sem
):
    parts, _, width = buf_ref.shape
    copies = weight_copies(w_hbm, chan_ref[0], buf_ref, in_sem)
    for copy in copies:
        copy.start()
    count = in_ref.shape[1] // 2
    mixing = in_ref[:, count:, :].astype(F32).reshape(ss_ref.shape) + ss_ref[...]
    gq_ref[...] = (mixing * gg_ref[...]).T.astype(BF16)
    write = pltpu.make_async_copy(gq_ref, gp_hbm.at[0], out_sem)
    write.start()
    for i, copy in enumerate(copies):
        copy.wait()
        out_ref[:, i * width : (i + 1) * width] = dot(gated_ref[...], buf_ref[i])
    write.wait()


def end_kernel(in_ref, sg_ref, proj_ref, gp_in, gp_hbm, gf_hbm, gp_ref, gf_ref, sem_ref):
    parts, _, rows, width = gp_ref.shape
    step, count = in_ref.shape[0] // parts, in_ref.shape[1] // 2
    writes = []
    for i in range(parts):
        at = slice(i * width, (i + 1) * width)
        block = in_ref[i * step : (i + 1) * step].astype(F32)
        gf_ref[i] = block[:, count:].reshape(width, rows).T
        gs = block[:, :count].reshape(width, rows).T + sg_ref[:, at]
        gp_ref[i, 0] = (gs * proj_ref[2, :, at].astype(F32)).astype(BF16)
        gp_ref[i, 1] = (gs * proj_ref[1, :, at].astype(F32)).astype(BF16)
        for source, target in (
            (gf_ref.at[i], gf_hbm.at[:, at]),
            (gp_ref.at[i], gp_hbm.at[1:3, :, at]),
        ):
            write = pltpu.make_async_copy(source, target, sem_ref.at[len(writes)])
            write.start()
            writes.append(write)
    for write in writes:
        write.wait()


VMEM = pl.BlockSpec(memory_space=pltpu.VMEM)
HBM = pl.BlockSpec(memory_space=pltpu.HBM)
SMEM = pl.BlockSpec(memory_space=pltpu.SMEM)


def conv_call(arrived, gm, tabs, each):
    blocks, _, rows = arrived.shape
    spec_shape = (each * blocks, 2 * rows)
    return pl.pallas_call(
        conv_kernel,
        in_specs=[VMEM, HBM] + [VMEM] * len(tabs),
        out_specs=[VMEM] * 2,
        out_shape=[
            jax.ShapeDtypeStruct((2,) + spec_shape, F32),
            jax.ShapeDtypeStruct(arrived.shape, BF16),
        ],
        scratch_shapes=[
            pltpu.VMEM((blocks * 2 * each, rows), F32),
            pltpu.VMEM(spec_shape, BF16),
            pltpu.VMEM(spec_shape, BF16),
            pltpu.VMEM(spec_shape, F32),
            pltpu.VMEM((blocks * each, rows), F32),
            pltpu.SemaphoreType.DMA(()),
        ],
        compiler_params=params(),
        name="conv",
    )(arrived, gm, *tabs)


def corr_call(back, spectra, tabs, each):
    blocks, _, rows = back.shape
    spec_shape = (each * blocks, 2 * rows)
    return pl.pallas_call(
        corr_kernel,
        in_specs=[VMEM] * (2 + len(tabs)),
        out_specs=VMEM,
        out_shape=jax.ShapeDtypeStruct(back.shape, BF16),
        scratch_shapes=[
            pltpu.VMEM((blocks * each, rows), F32),
            pltpu.VMEM(spec_shape, BF16),
            pltpu.VMEM(spec_shape, BF16),
            pltpu.VMEM(spec_shape, F32),
            pltpu.VMEM(spec_shape, F32),
            pltpu.VMEM((blocks * 2 * each, rows), F32),
        ],
        compiler_params=params(),
        name="corr",
    )(back, spectra, *tabs)


def local(projected, skip_gain, out_weight, long_filter, cotangent):
    blocks = lax.axis_size("seq")
    rows, channels = long_filter.shape
    each = channels // blocks
    width = out_weight.shape[1]
    half = width // 2
    chan = lax.axis_index("chan").astype(jnp.int32).reshape(1)
    in_hbm = lambda x: pltpu.with_memory_space_constraint(x, pltpu.HBM)
    proj = in_hbm(projected.transpose(1, 0, 2))
    out_weight = in_hbm(out_weight)
    long_filter = in_hbm(long_filter)
    skip = skip_gain.reshape(1, channels)
    tabs = [jnp.asarray(t) for t in tables(blocks, rows)]
    full = lambda shape: pl.BlockSpec(shape, lambda *_: (0,) * len(shape))
    shape = jax.ShapeDtypeStruct

    other = lax.ppermute(cotangent, "chan", [(0, 1), (1, 0)])

    def exchange(x):
        return lax.all_to_all(x, "seq", 0, 0, tiled=True)

    smem, vmem, hbm = SMEM, VMEM, HBM
    parts = 4
    cb = channels // parts
    pb = blocks // parts
    signals = pl.pallas_call(
        prep_kernel,
        in_specs=[hbm, hbm],
        out_specs=hbm,
        out_shape=shape((blocks, 2 * each, rows), BF16),
        scratch_shapes=[
            pltpu.VMEM((parts, 2, rows, cb), BF16),
            pltpu.VMEM((parts, rows, cb), F32),
            pltpu.VMEM((parts, pb, 2 * each, rows), BF16),
            pltpu.SemaphoreType.DMA((parts, 2)),
            pltpu.SemaphoreType.DMA((parts,)),
        ],
        compiler_params=params(),
        name="prep",
    )(proj, long_filter)
    arrived = exchange(signals)

    gm, query, gg, skip_source, skip_grad = pl.pallas_call(
        grad_kernel,
        grid_spec=pltpu.PrefetchScalarGridSpec(
            num_scalar_prefetch=1,
            grid=(parts,),
            in_specs=[
                pl.BlockSpec((cb, width), lambda i, c: (i, 0)),
                full((rows, half)),
                full((rows, half)),
                pl.BlockSpec((3, rows, cb), lambda i, c: (0, 0, i)),
                pl.BlockSpec((1, cb), lambda i, c: (0, i)),
            ],
            out_specs=[pl.BlockSpec((cb, rows), lambda i, c: (i, 0))] * 4
            + [pl.BlockSpec((rows, cb), lambda i, c: (0, i))],
        ),
        out_shape=[shape((channels, rows), BF16)] * 2
        + [shape((channels, rows), F32)] * 2
        + [shape((rows, channels), F32)],
        compiler_params=params(),
        cost_estimate=pl.CostEstimate(flops=10**11, transcendentals=0, bytes_accessed=10**9),
        name="grad",
    )(chan, out_weight, cotangent, other, proj, skip)

    spectra, mid = conv_call(arrived, in_hbm(gm.reshape(blocks, each, rows)), tabs, each)
    back = exchange(mid)

    pair = corr_call(back, spectra, tabs, each)
    last = exchange(pair)

    pieces = 4
    wb = half // pieces
    weights = pltpu.VMEM((pieces, channels, wb), BF16)
    sems = pltpu.SemaphoreType.DMA((pieces,))
    send, gated = pl.pallas_call(
        mix_kernel,
        in_specs=[smem, vmem, vmem, vmem, hbm],
        out_specs=[hbm, vmem],
        out_shape=[pltpu.HBM((rows, half), BF16), shape((rows, channels), BF16)],
        scratch_shapes=[weights, pltpu.VMEM((pieces, rows, wb), BF16), sems, sems],
        compiler_params=params(),
        name="mix",
    )(chan, back, skip_source, query, out_weight)
    received = lax.ppermute(send, "chan", [(0, 1), (1, 0)])
    kept, stacked = pl.pallas_call(
        own_kernel,
        in_specs=[smem, vmem, vmem, vmem, vmem, hbm],
        out_specs=[vmem, hbm],
        out_shape=[shape((rows, half), F32), pltpu.HBM((3, rows, channels), BF16)],
        scratch_shapes=[
            weights,
            pltpu.VMEM((rows, channels), BF16),
            sems,
            pltpu.SemaphoreType.DMA(()),
        ],
        compiler_params=params(),
        name="own",
    )(chan, back, skip_source, in_hbm(gg), gated, out_weight)
    mixed = (kept + received.astype(F32)).astype(BF16)

    grad_projected, grad_filter = pl.pallas_call(
        end_kernel,
        in_specs=[vmem, vmem, vmem, hbm],
        out_specs=[hbm] * 2,
        out_shape=[shape((3, rows, channels), BF16), shape((rows, channels), F32)],
        scratch_shapes=[
            pltpu.VMEM((parts, 2, rows, cb), BF16),
            pltpu.VMEM((parts, rows, cb), F32),
            pltpu.SemaphoreType.DMA((2 * parts,)),
        ],
        input_output_aliases={3: 0},
        compiler_params=params(),
        name="end",
    )(last, skip_grad, projected.transpose(1, 0, 2), stacked)
    return mixed, grad_projected.transpose(1, 0, 2), grad_filter


def solution(mesh):
    in_specs = (
        P("seq", None, "chan"),
        P("chan"),
        P("chan", None),
        P("seq", "chan"),
        P("seq", "chan"),
    )
    out_specs = (P("seq", "chan"), P("seq", None, "chan"), P("seq", "chan"))
    return jax.shard_map(local, mesh=mesh, in_specs=in_specs, out_specs=out_specs, check_vma=False)
```

```python
import math

import jax
import jax.numpy as jnp
import numpy as np
from jax import lax
from jax.experimental import pallas as pl
from jax.experimental.pallas import tpu as pltpu
from jax.sharding import PartitionSpec as P

F32 = jnp.float32
BF16 = jnp.bfloat16
VMEM_LIMIT = 20 * 1024 * 1024
GAIN = 1.6657
COSTLY = pl.CostEstimate(flops=10**11, transcendentals=0, bytes_accessed=10**9)


def params():
    return pltpu.CompilerParams(vmem_limit_bytes=VMEM_LIMIT)


def halves(table):
    high = table.astype(BF16)
    low = (table - high.astype(np.float64)).astype(BF16)
    return high, low


def tables(blocks, rows):
    length = 2 * blocks * rows
    k1 = np.arange(blocks)[:, None] + 0.5
    angle = 2.0 * np.pi * k1 * np.arange(blocks)[None, :] / (2 * blocks)
    outer = np.concatenate([np.cos(angle), -np.sin(angle)], axis=0)
    outer_high, outer_low = halves(outer)
    outer_both = np.concatenate([outer_high, outer_low], axis=1)
    back_both = np.concatenate(halves(outer.T), axis=0)
    order = np.arange(blocks).reshape(blocks // 2, 2).T.reshape(-1)
    outer_order = np.concatenate([outer_high[:, order], outer_low[:, order]], axis=1)
    back_order = np.concatenate(halves(outer.T[order]), axis=0)
    turn = 2.0 * np.pi * k1 * np.arange(rows)[None, :] / length
    turn_re = np.cos(turn).astype(np.float32)
    turn_im = -np.sin(turn).astype(np.float32)
    grid = 2.0 * np.pi * (np.outer(np.arange(rows), np.arange(rows)) % rows) / rows
    cos, sin = np.cos(grid), np.sin(grid)
    inner = GAIN * np.block([[cos, -sin], [sin, cos]])
    shared = [turn_re, turn_im, inner.astype(BF16), inner.T.astype(BF16)]
    return [outer_both, back_order, *shared], [outer_order, back_both, *shared]


def dot(a, b):
    return jnp.dot(a, b, preferred_element_type=F32)


def transform(high_ref, low_ref, table):
    return dot(high_ref[...], table[...]) + dot(low_ref[...], table[...])


def dot_t(a, b):
    return lax.dot_general(a, b, (((1,), (1,)), ((), ())), preferred_element_type=F32)


def split(x):
    high = x.astype(BF16)
    return high, (x - high.astype(F32)).astype(BF16)


def forward(load, blocks, rows, count, tabs, high_ref, low_ref, spec_ref):
    outer, _, turn_re, turn_im, inner, _ = tabs
    tre, tim = turn_re[...], turn_im[...]
    for pair in range(count // 2):
        x = jnp.concatenate([load(2 * pair + j).astype(BF16) for j in range(2)], axis=1)
        a = dot(outer[...], jnp.concatenate([x, x], axis=0))
        for j in range(2):
            are = a[:blocks, j * rows : (j + 1) * rows]
            aim = a[blocks:, j * rows : (j + 1) * rows]
            b = jnp.concatenate([are * tre - aim * tim, are * tim + aim * tre], axis=1)
            high, low = split(b)
            at = (2 * pair + j) * blocks
            high_ref[at : at + blocks, :] = high
            low_ref[at : at + blocks, :] = low
    spec_ref[...] = transform(high_ref, low_ref, inner)


def inverse(high_ref, low_ref, part_ref, tabs, scale, blocks, rows, count, store):
    _, back_both, turn_re, turn_im, _, inner = tabs
    scale /= GAIN**3
    tre, tim = turn_re[...] * scale, turn_im[...] * scale
    part_ref[...] = transform(high_ref, low_ref, inner)
    for pair in range(count // 2):
        both = []
        for j in range(2):
            at = (2 * pair + j) * blocks
            cre = part_ref[at : at + blocks, :rows]
            cim = part_ref[at : at + blocks, rows:]
            both.append(jnp.concatenate([cre * tre + cim * tim, cim * tre - cre * tim], axis=0))
        high, low = split(jnp.concatenate(both, axis=1))
        y = dot(back_both[...], high)
        y = y[:blocks] + y[blocks:] + dot(back_both[:blocks, :], low)
        for j in range(2):
            store(2 * pair + j, y[:, j * rows : (j + 1) * rows])


def product(a_ref, b_ref, conj, high_ref, low_ref):
    half = a_ref.shape[1] // 2
    total = a_ref.shape[0]
    step = total // 8
    for i in range(8):
        at = slice(i * step, (i + 1) * step)
        ar, ai = a_ref[at, :half], a_ref[at, half:]
        br, bi = b_ref[at, :half], b_ref[at, half:]
        if conj:
            z = jnp.concatenate([ar * br + ai * bi, ar * bi - ai * br], axis=1)
        else:
            z = jnp.concatenate([ar * br - ai * bi, ar * bi + ai * br], axis=1)
        high, low = split(z)
        high_ref[at, :] = high
        low_ref[at, :] = low


def prep_kernel(proj_hbm, filter_hbm, out_hbm, pair_ref, filter_ref, out_ref, in_sem, out_sem):
    parts, _, rows, width = pair_ref.shape
    step, each = out_ref.shape[1], out_ref.shape[2] // 2
    reads, writes = [], []
    for i in range(parts):
        at = slice(i * width, (i + 1) * width)
        reads.append(
            (
                pltpu.make_async_copy(proj_hbm.at[1:3, :, at], pair_ref.at[i], in_sem.at[i, 0]),
                pltpu.make_async_copy(filter_hbm.at[:, at], filter_ref.at[i], in_sem.at[i, 1]),
            )
        )
        writes.append(
            pltpu.make_async_copy(
                out_ref.at[i], out_hbm.at[i * step : (i + 1) * step], out_sem.at[i]
            )
        )
    for pair, taps in reads:
        pair.start()
        taps.start()
    for i in range(parts):
        pair, taps = reads[i]
        pair.wait()
        source = pair_ref[i, 0].astype(F32) * pair_ref[i, 1].astype(F32)
        out_ref[i, :, :each, :] = source.T.reshape(step, each, rows).astype(BF16)
        taps.wait()
        out_ref[i, :, each:, :] = filter_ref[i].T.reshape(step, each, rows).astype(BF16)
        writes[i].start()
    for write in writes:
        write.wait()


def slot_of(near, place_ref):
    return near ^ place_ref[1]


def grad_kernel(
    place_ref, w_ref, own_ref, other_ref, proj_ref, skip_ref,
    q_ref, gg_ref, ss_ref, sg_ref, *rest,
):
    pieces, (gm_ref, sem_ref) = rest[:2], rest[2:]
    half = own_ref.shape[1]
    first = place_ref[0] == 0
    own, other = own_ref[...], other_ref[...]
    low = jnp.where(first, own, other)
    high = jnp.where(first, other, own)
    gg = dot_t(w_ref[:, :half], low) + dot_t(w_ref[:, half:], high)
    query = proj_ref[0].astype(F32).T
    gm = gg * query
    skip = skip_ref[...]
    gg_ref[...] = gg
    q_ref[...] = query.astype(BF16)
    step = pl.program_id(0)
    wide = gm.reshape(gm_ref.shape[2], 2, gm_ref.shape[3], gm.shape[1])
    for near in range(2):
        gm_ref[step, near] = wide[:, near].astype(BF16)
    sg_ref[...] = gm.T * skip
    ss_ref[...] = (proj_ref[1].astype(F32) * proj_ref[2].astype(F32) * skip).T
    steps, _, span = gm_ref.shape[:3]

    def copies(i, act):
        at = i * span
        for near in range(2):
            for k in range(2):

                @pl.when(slot_of(near, place_ref) == k)
                def _():
                    act(
                        pltpu.make_async_copy(
                            gm_ref.at[i, near], pieces[k].at[at : at + span], sem_ref.at[i, near]
                        )
                    )

    for i in range(steps):

        @pl.when(step == i)
        def _():
            copies(i, lambda copy: copy.start())

    @pl.when(step == steps - 1)
    def _():
        for i in range(steps):
            copies(i, lambda copy: copy.wait())


def conv_kernel(*refs):
    place_ref, in_ref = refs[:2]
    gm_refs, tabs = refs[2:4], refs[4:10]
    spec_ref, out_ref = refs[10:12]
    wide_ref, high_ref, low_ref, part_ref, back_ref, gm_sem = refs[12:]
    blocks, two, rows = in_ref.shape
    count = two // 2
    middle = blocks // 2
    copies = [
        pltpu.make_async_copy(
            gm_refs[k], out_ref.at[:, k * count : (k + 1) * count, :], gm_sem.at[k]
        )
        for k in range(2)
    ]
    for copy in copies:
        copy.start()
    wide_ref[...] = in_ref[...].astype(F32).reshape(blocks * two, rows)
    for s in range(2):

        def load(c):
            return wide_ref[pl.ds(s * count + c, blocks, stride=two), :]

        forward(load, blocks, rows, count, tabs, high_ref, low_ref, spec_ref.at[s])
    product(spec_ref.at[0], spec_ref.at[1], False, high_ref, low_ref)

    def store(c, y):
        for near in range(2):
            at = slot_of(near, place_ref) * count + c
            back_ref[pl.ds(at, middle, stride=2 * count), :] = y[near * middle : (near + 1) * middle]

    inverse(high_ref, low_ref, part_ref, tabs, 1.0 / (blocks * rows), blocks, rows, count, store)
    for copy in copies:
        copy.wait()
    out_ref[:, 2 * count :, :] = back_ref[...].reshape(middle, 2 * count, rows).astype(BF16)


def corr_kernel(*refs):
    place_ref, in_ref, spec_ref = refs[:3]
    tabs = refs[3:9]
    out_ref, piece = refs[9:11]
    wide_ref, high_ref, low_ref, part_ref, grad_ref, back_ref, sem = refs[11:]
    blocks, two, rows = out_ref.shape
    count = two // 2
    middle = blocks // 2
    copy = pltpu.make_async_copy(in_ref.at[:, 3 * count :, :], piece, sem)
    copy.start()
    wide_ref[...] = in_ref[:, : 2 * count, :].astype(F32).reshape(middle * 2 * count, rows)

    def load(c):
        return jnp.concatenate(
            [
                wide_ref[pl.ds(slot_of(near, place_ref) * count + c, middle, stride=2 * count), :]
                for near in range(2)
            ],
            axis=0,
        )

    forward(load, blocks, rows, count, tabs, high_ref, low_ref, grad_ref)
    scale = 1.0 / (blocks * rows)
    for s, factor in ((1, scale), (0, scale / math.sqrt(blocks * rows))):

        def store(c, y):
            back_ref[pl.ds((1 - s) * count + c, blocks, stride=two), :] = y

        product(spec_ref.at[s], grad_ref, True, high_ref, low_ref)
        inverse(high_ref, low_ref, part_ref, tabs, factor, blocks, rows, count, store)
    out_ref[...] = back_ref[...].reshape(blocks, two, rows).astype(BF16)
    copy.wait()


def weight_copies(w_hbm, chan, buf_ref, sem_ref):
    parts, _, width = buf_ref.shape
    return [
        pltpu.make_async_copy(
            w_hbm.at[:, pl.ds(pl.multiple_of((chan * parts + i) * width, width), width)],
            buf_ref.at[i],
            sem_ref.at[i],
        )
        for i in range(parts)
    ]


def mix_kernel(
    place_ref, in_ref, *refs
):
    other_ref, ss_ref, q_ref, w_hbm, send_hbm, gated_ref, mixing_ref = refs[:7]
    all_ref, buf_ref, send_ref, in_sem, out_sem = refs[7:]
    parts, _, width = buf_ref.shape
    copies = weight_copies(w_hbm, 1 - place_ref[0], buf_ref, in_sem)
    for copy in copies:
        copy.start()
    count = in_ref.shape[1] // 4
    all_ref[:, place_ref[1]] = in_ref[:, 2 * count : 3 * count, :].astype(F32)
    all_ref[:, 1 - place_ref[1]] = other_ref[...].astype(F32)
    mixing = all_ref[...].reshape(ss_ref.shape) + ss_ref[...]
    mixing_ref[...] = mixing
    gated_ref[...] = (mixing * q_ref[...].astype(F32)).T.astype(BF16)
    writes = []
    for i, copy in enumerate(copies):
        copy.wait()
        send_ref[i] = dot(gated_ref[...], buf_ref[i]).astype(BF16)
        write = pltpu.make_async_copy(
            send_ref.at[i], send_hbm.at[:, i * width : (i + 1) * width], out_sem.at[i]
        )
        write.start()
        writes.append(write)
    for write in writes:
        write.wait()


def own_kernel(
    place_ref, mixing_ref, gg_ref, gated_ref, w_hbm, out_ref, gp_hbm, buf_ref, gq_ref, in_sem, out_sem
):
    parts, _, width = buf_ref.shape
    copies = weight_copies(w_hbm, place_ref[0], buf_ref, in_sem)
    for copy in copies:
        copy.start()
    gq_ref[...] = (mixing_ref[...] * gg_ref[...]).T.astype(BF16)
    write = pltpu.make_async_copy(gq_ref, gp_hbm.at[0], out_sem)
    write.start()
    for i, copy in enumerate(copies):
        copy.wait()
        out_ref[:, i * width : (i + 1) * width] = dot(gated_ref[...], buf_ref[i])
    write.wait()


def end_kernel(in_ref, sg_ref, proj_ref, gp_in, gp_hbm, gf_hbm, gp_ref, gf_ref, sem_ref):
    parts, _, rows, width = gp_ref.shape
    step, count = in_ref.shape[0] // parts, in_ref.shape[1] // 2
    writes = []
    for i in range(parts):
        at = slice(i * width, (i + 1) * width)
        block = in_ref[i * step : (i + 1) * step].astype(F32)
        gf_ref[i] = block[:, count:].reshape(width, rows).T
        gs = block[:, :count].reshape(width, rows).T + sg_ref[:, at]
        gp_ref[i, 0] = (gs * proj_ref[2, :, at].astype(F32)).astype(BF16)
        gp_ref[i, 1] = (gs * proj_ref[1, :, at].astype(F32)).astype(BF16)
        for source, target in (
            (gf_ref.at[i], gf_hbm.at[:, at]),
            (gp_ref.at[i], gp_hbm.at[1:3, :, at]),
        ):
            write = pltpu.make_async_copy(source, target, sem_ref.at[len(writes)])
            write.start()
            writes.append(write)
    for write in writes:
        write.wait()


VMEM = pl.BlockSpec(memory_space=pltpu.VMEM)
HBM = pl.BlockSpec(memory_space=pltpu.HBM)
SMEM = pl.BlockSpec(memory_space=pltpu.SMEM)


def conv_call(place, arrived, gm, tabs, each):
    blocks, _, rows = arrived.shape
    middle = blocks // 2
    spec_shape = (each * blocks, 2 * rows)
    return pl.pallas_call(
        conv_kernel,
        in_specs=[SMEM, VMEM] + [HBM] * 2 + [VMEM] * len(tabs),
        out_specs=[VMEM] * 2,
        out_shape=[
            jax.ShapeDtypeStruct((2,) + spec_shape, F32),
            jax.ShapeDtypeStruct((middle, 4 * each, rows), BF16),
        ],
        scratch_shapes=[
            pltpu.VMEM((blocks * 2 * each, rows), F32),
            pltpu.VMEM(spec_shape, BF16),
            pltpu.VMEM(spec_shape, BF16),
            pltpu.VMEM(spec_shape, F32),
            pltpu.VMEM((blocks * each, rows), F32),
            pltpu.SemaphoreType.DMA((2,)),
        ],
        compiler_params=params(),
        name="conv",
    )(place, arrived, *gm, *tabs)


def corr_call(place, back, spectra, tabs, each):
    middle, _, rows = back.shape
    blocks = 2 * middle
    spec_shape = (each * blocks, 2 * rows)
    return pl.pallas_call(
        corr_kernel,
        in_specs=[SMEM] + [VMEM] * (2 + len(tabs)),
        out_specs=[VMEM, HBM],
        out_shape=[jax.ShapeDtypeStruct((blocks, 2 * each, rows), BF16)]
        + [pltpu.HBM((middle, each, rows), BF16)],
        scratch_shapes=[
            pltpu.VMEM((blocks * each, rows), F32),
            pltpu.VMEM(spec_shape, BF16),
            pltpu.VMEM(spec_shape, BF16),
            pltpu.VMEM(spec_shape, F32),
            pltpu.VMEM(spec_shape, F32),
            pltpu.VMEM((blocks * 2 * each, rows), F32),
            pltpu.SemaphoreType.DMA(()),
        ],
        compiler_params=params(),
        cost_estimate=COSTLY,
        name="corr",
    )(place, back, spectra, *tabs)


def local(projected, skip_gain, out_weight, long_filter, cotangent):
    blocks = lax.axis_size("seq")
    rows, channels = long_filter.shape
    each = channels // blocks
    width = out_weight.shape[1]
    half = width // 2
    seq = lax.axis_index("seq").astype(jnp.int32)
    middle = blocks // 2
    place = jnp.stack([lax.axis_index("chan").astype(jnp.int32), seq % 2])
    in_hbm = lambda x: pltpu.with_memory_space_constraint(x, pltpu.HBM)
    proj = in_hbm(projected.transpose(1, 0, 2))
    out_weight = in_hbm(out_weight)
    long_filter = in_hbm(long_filter)
    skip = skip_gain.reshape(1, channels)
    tabs_conv, tabs_corr = tables(blocks, rows)
    chips = [[2 * m + near for m in range(middle)] for near in range(2)]

    def partner(x):
        return lax.ppermute(x, "seq", [(i, i ^ 1) for i in range(blocks)])

    in_hbm = lambda x: pltpu.with_memory_space_constraint(x, pltpu.HBM)
    proj = in_hbm(projected.transpose(1, 0, 2))
    out_weight = in_hbm(out_weight)
    long_filter = in_hbm(long_filter)
    skip = skip_gain.reshape(1, channels)
    full = lambda shape: pl.BlockSpec(shape, lambda *_: (0,) * len(shape))
    shape = jax.ShapeDtypeStruct

    other = lax.ppermute(cotangent, "chan", [(0, 1), (1, 0)])

    def exchange(x):
        return lax.all_to_all(x, "seq", 0, 0, tiled=True)

    smem, vmem, hbm = SMEM, VMEM, HBM
    parts = 4
    cb = channels // parts
    pb = blocks // parts
    signals = pl.pallas_call(
        prep_kernel,
        in_specs=[hbm, hbm],
        out_specs=hbm,
        out_shape=shape((blocks, 2 * each, rows), BF16),
        scratch_shapes=[
            pltpu.VMEM((parts, 2, rows, cb), BF16),
            pltpu.VMEM((parts, rows, cb), F32),
            pltpu.VMEM((parts, pb, 2 * each, rows), BF16),
            pltpu.SemaphoreType.DMA((parts, 2)),
            pltpu.SemaphoreType.DMA((parts,)),
        ],
        compiler_params=params(),
        name="prep",
    )(proj, long_filter)
    arrived = exchange(signals)

    span = cb // (2 * each)
    query, gg, skip_source, skip_grad, gm_own, gm_give = pl.pallas_call(
        grad_kernel,
        grid_spec=pltpu.PrefetchScalarGridSpec(
            num_scalar_prefetch=1,
            grid=(parts,),
            in_specs=[
                pl.BlockSpec((cb, width), lambda i, c: (i, 0)),
                full((rows, half)),
                full((rows, half)),
                pl.BlockSpec((3, rows, cb), lambda i, c: (0, 0, i)),
                pl.BlockSpec((1, cb), lambda i, c: (0, i)),
            ],
            out_specs=[pl.BlockSpec((cb, rows), lambda i, c: (i, 0))] * 3
            + [pl.BlockSpec((rows, cb), lambda i, c: (0, i))]
            + [hbm] * 2,
            scratch_shapes=[
                pltpu.VMEM((parts, 2, span, each, rows), BF16),
                pltpu.SemaphoreType.DMA((parts, 2)),
            ],
        ),
        out_shape=[shape((channels, rows), BF16)]
        + [shape((channels, rows), F32)] * 2
        + [shape((rows, channels), F32)]
        + [pltpu.HBM((middle, each, rows), BF16)] * 2,
        compiler_params=params(),
        cost_estimate=COSTLY,
        name="grad",
    )(place, out_weight, in_hbm(cotangent), in_hbm(other), proj, skip)
    gm = [in_hbm(gm_own), partner(gm_give)]

    spectra, mid = conv_call(place, arrived, gm, tabs_conv, each)
    back = lax.all_to_all(mid, "seq", 0, 0, tiled=True, axis_index_groups=chips)
    pair, conv_give = corr_call(place, back, spectra, tabs_corr, each)
    conv_got = partner(conv_give)
    last = exchange(pair)

    pieces = 4
    wb = half // pieces
    weights = pltpu.VMEM((pieces, channels, wb), BF16)
    sems = pltpu.SemaphoreType.DMA((pieces,))
    send, gated, mixing = pl.pallas_call(
        mix_kernel,
        in_specs=[smem] + [vmem] * 4 + [hbm],
        out_specs=[hbm, vmem, vmem],
        out_shape=[
            pltpu.HBM((rows, half), BF16),
            shape((rows, channels), BF16),
            shape((channels, rows), F32),
        ],
        scratch_shapes=[
            pltpu.VMEM((middle, 2, each, rows), F32),
            weights,
            pltpu.VMEM((pieces, rows, wb), BF16),
            sems,
            sems,
        ],
        compiler_params=params(),
        cost_estimate=COSTLY,
        name="mix",
    )(place, back, conv_got, skip_source, query, out_weight)
    received = lax.ppermute(send, "chan", [(0, 1), (1, 0)])
    kept, stacked = pl.pallas_call(
        own_kernel,
        in_specs=[smem, vmem, vmem, vmem, hbm],
        out_specs=[vmem, hbm],
        out_shape=[shape((rows, half), F32), pltpu.HBM((3, rows, channels), BF16)],
        scratch_shapes=[
            weights,
            pltpu.VMEM((rows, channels), BF16),
            sems,
            pltpu.SemaphoreType.DMA(()),
        ],
        compiler_params=params(),
        name="own",
    )(place, mixing, in_hbm(gg), gated, out_weight)
    mixed = (kept + received.astype(F32)).astype(BF16)

    grad_projected, grad_filter = pl.pallas_call(
        end_kernel,
        in_specs=[vmem, vmem, vmem, hbm],
        out_specs=[hbm] * 2,
        out_shape=[shape((3, rows, channels), BF16), shape((rows, channels), F32)],
        scratch_shapes=[
            pltpu.VMEM((parts, 2, rows, cb), BF16),
            pltpu.VMEM((parts, rows, cb), F32),
            pltpu.SemaphoreType.DMA((2 * parts,)),
        ],
        input_output_aliases={3: 0},
        compiler_params=params(),
        name="end",
    )(last, skip_grad, projected.transpose(1, 0, 2), stacked)
    return mixed, grad_projected.transpose(1, 0, 2), grad_filter


def solution(mesh):
    in_specs = (
        P("seq", None, "chan"),
        P("chan"),
        P("chan", None),
        P("seq", "chan"),
        P("seq", "chan"),
    )
    out_specs = (P("seq", "chan"), P("seq", None, "chan"), P("seq", "chan"))
    return jax.shard_map(local, mesh=mesh, in_specs=in_specs, out_specs=out_specs, check_vma=False)
```

```python
import math

import jax
import jax.numpy as jnp
import numpy as np
from jax import lax
from jax.experimental import pallas as pl
from jax.experimental.pallas import tpu as pltpu
from jax.sharding import PartitionSpec as P

F32 = jnp.float32
BF16 = jnp.bfloat16
VMEM_LIMIT = 20 * 1024 * 1024
GAIN = 1.6657
COSTLY = pl.CostEstimate(flops=10**11, transcendentals=0, bytes_accessed=10**9)


def params():
    return pltpu.CompilerParams(vmem_limit_bytes=VMEM_LIMIT)


def halves(table):
    high = table.astype(BF16)
    low = (table - high.astype(np.float64)).astype(BF16)
    return high, low


def tables(blocks, rows):
    length = 2 * blocks * rows
    k1 = np.arange(blocks)[:, None] + 0.5
    angle = 2.0 * np.pi * k1 * np.arange(blocks)[None, :] / (2 * blocks)
    outer = np.concatenate([np.cos(angle), -np.sin(angle)], axis=0)
    outer_high, outer_low = halves(outer)
    outer_both = np.concatenate([outer_high, outer_low], axis=1)
    back_both = np.concatenate(halves(outer.T), axis=0)
    even = np.arange(blocks).reshape(blocks // 2, 2).T.reshape(-1)
    orders = [even, np.roll(even, blocks // 2)]
    outer_order = np.stack([np.concatenate([outer_high[:, o], outer_low[:, o]], 1) for o in orders])
    back_order = np.stack([np.concatenate(halves(outer.T[o]), axis=0) for o in orders])
    turn = 2.0 * np.pi * k1 * np.arange(rows)[None, :] / length
    turn_re = np.cos(turn).astype(np.float32)
    turn_im = -np.sin(turn).astype(np.float32)
    grid = 2.0 * np.pi * (np.outer(np.arange(rows), np.arange(rows)) % rows) / rows
    cos, sin = np.cos(grid), np.sin(grid)
    inner = GAIN * np.block([[cos, -sin], [sin, cos]])
    shared = [turn_re, turn_im, inner.astype(BF16), inner.T.astype(BF16)]
    return [outer_both, back_order, *shared], [outer_order, back_both, *shared]


def dot(a, b):
    return jnp.dot(a, b, preferred_element_type=F32)


def transform(high_ref, low_ref, table):
    return dot(high_ref[...], table[...]) + dot(low_ref[...], table[...])


def dot_t(a, b):
    return lax.dot_general(a, b, (((1,), (1,)), ((), ())), preferred_element_type=F32)


def split(x):
    high = x.astype(BF16)
    return high, (x - high.astype(F32)).astype(BF16)


def forward(load, blocks, rows, count, tabs, high_ref, low_ref, spec_ref):
    outer, _, turn_re, turn_im, inner, _ = tabs
    tre, tim = turn_re[...], turn_im[...]
    for pair in range(count // 2):
        x = jnp.concatenate([load(2 * pair + j).astype(BF16) for j in range(2)], axis=1)
        a = dot(outer[...], jnp.concatenate([x, x], axis=0))
        for j in range(2):
            are = a[:blocks, j * rows : (j + 1) * rows]
            aim = a[blocks:, j * rows : (j + 1) * rows]
            b = jnp.concatenate([are * tre - aim * tim, are * tim + aim * tre], axis=1)
            high, low = split(b)
            at = (2 * pair + j) * blocks
            high_ref[at : at + blocks, :] = high
            low_ref[at : at + blocks, :] = low
    spec_ref[...] = transform(high_ref, low_ref, inner)


def inverse(high_ref, low_ref, part_ref, tabs, scale, blocks, rows, count, store):
    _, back_both, turn_re, turn_im, _, inner = tabs
    scale /= GAIN**3
    tre, tim = turn_re[...] * scale, turn_im[...] * scale
    part_ref[...] = transform(high_ref, low_ref, inner)
    for pair in range(count // 2):
        both = []
        for j in range(2):
            at = (2 * pair + j) * blocks
            cre = part_ref[at : at + blocks, :rows]
            cim = part_ref[at : at + blocks, rows:]
            both.append(jnp.concatenate([cre * tre + cim * tim, cim * tre - cre * tim], axis=0))
        high, low = split(jnp.concatenate(both, axis=1))
        y = dot(back_both[...], high)
        y = y[:blocks] + y[blocks:] + dot(back_both[:blocks, :], low)
        for j in range(2):
            store(2 * pair + j, y[:, j * rows : (j + 1) * rows])


def product(a_ref, b_ref, conj, high_ref, low_ref):
    half = a_ref.shape[1] // 2
    total = a_ref.shape[0]
    step = total // 8
    for i in range(8):
        at = slice(i * step, (i + 1) * step)
        ar, ai = a_ref[at, :half], a_ref[at, half:]
        br, bi = b_ref[at, :half], b_ref[at, half:]
        if conj:
            z = jnp.concatenate([ar * br + ai * bi, ar * bi - ai * br], axis=1)
        else:
            z = jnp.concatenate([ar * br - ai * bi, ar * bi + ai * br], axis=1)
        high, low = split(z)
        high_ref[at, :] = high
        low_ref[at, :] = low


def prep_kernel(proj_hbm, filter_hbm, out_hbm, pair_ref, filter_ref, out_ref, in_sem, out_sem):
    parts, _, rows, width = pair_ref.shape
    step, each = out_ref.shape[1], out_ref.shape[2] // 2
    reads, writes = [], []
    for i in range(parts):
        at = slice(i * width, (i + 1) * width)
        reads.append(
            (
                pltpu.make_async_copy(proj_hbm.at[1:3, :, at], pair_ref.at[i], in_sem.at[i, 0]),
                pltpu.make_async_copy(filter_hbm.at[:, at], filter_ref.at[i], in_sem.at[i, 1]),
            )
        )
        writes.append(
            pltpu.make_async_copy(
                out_ref.at[i], out_hbm.at[i * step : (i + 1) * step], out_sem.at[i]
            )
        )
    for pair, taps in reads:
        pair.start()
        taps.start()
    for i in range(parts):
        pair, taps = reads[i]
        pair.wait()
        source = pair_ref[i, 0].astype(F32) * pair_ref[i, 1].astype(F32)
        out_ref[i, :, :each, :] = source.T.reshape(step, each, rows).astype(BF16)
        taps.wait()
        out_ref[i, :, each:, :] = filter_ref[i].T.reshape(step, each, rows).astype(BF16)
        writes[i].start()
    for write in writes:
        write.wait()


def core():
    return lax.axis_index("seq") & 1


def grad_kernel(
    w_ref, own_ref, other_ref, proj_ref, skip_ref,
    q_ref, gg_ref, ss_ref, sg_ref, *rest,
):
    pieces, (gm_ref, sem_ref) = rest[:2], rest[2:]
    half = own_ref.shape[1]
    first = lax.axis_index("chan") == 0
    own, other = own_ref[...], other_ref[...]
    low = jnp.where(first, own, other)
    high = jnp.where(first, other, own)
    gg = dot_t(w_ref[:, :half], low) + dot_t(w_ref[:, half:], high)
    query = proj_ref[0].astype(F32).T
    gm = gg * query
    skip = skip_ref[...]
    gg_ref[...] = gg
    q_ref[...] = query.astype(BF16)
    step = pl.program_id(0)
    wide = gm.reshape(gm_ref.shape[2], 2, gm_ref.shape[3], gm.shape[1])
    for near in range(2):
        gm_ref[step, near] = wide[:, near].astype(BF16)
    sg_ref[...] = gm.T * skip
    ss_ref[...] = (proj_ref[1].astype(F32) * proj_ref[2].astype(F32) * skip).T
    steps, _, span = gm_ref.shape[:3]

    def copies(i, act):
        at = i * span
        for near in range(2):
            for k in range(2):

                @pl.when(near ^ core() == k)
                def _():
                    act(
                        pltpu.make_async_copy(
                            gm_ref.at[i, near], pieces[k].at[at : at + span], sem_ref.at[i, near]
                        )
                    )

    for i in range(steps):

        @pl.when(step == i)
        def _():
            copies(i, lambda copy: copy.start())

    @pl.when(step == steps - 1)
    def _():
        for i in range(steps):
            copies(i, lambda copy: copy.wait())


def conv_kernel(*refs):
    in_ref, gm_refs, tabs = refs[0], refs[1:3], refs[3:9]
    spec_ref, out_ref = refs[9:11]
    wide_ref, high_ref, low_ref, part_ref, back_ref, gm_sem = refs[11:]
    blocks, two, rows = in_ref.shape
    count = two // 2
    middle = blocks // 2
    copies = [
        pltpu.make_async_copy(
            gm_refs[k], out_ref.at[:, k * count : (k + 1) * count, :], gm_sem.at[k]
        )
        for k in range(2)
    ]
    for copy in copies:
        copy.start()
    for s in range(2):
        wide_ref[s] = in_ref[:, s * count : (s + 1) * count, :].astype(F32).reshape(-1, rows)

        def load(c):
            return wide_ref[s, pl.ds(c, blocks, stride=count), :]

        forward(load, blocks, rows, count, tabs, high_ref, low_ref, spec_ref.at[s])
    product(spec_ref.at[0], spec_ref.at[1], False, high_ref, low_ref)

    def store(c, y):
        back_ref[pl.ds(c, blocks, stride=count), :] = y

    mine = (tabs[0], tabs[1].at[core()], *tabs[2:])
    inverse(high_ref, low_ref, part_ref, mine, 1.0 / (blocks * rows), blocks, rows, count, store)
    for copy in copies:
        copy.wait()
    for k in range(2):
        part = back_ref[k * middle * count : (k + 1) * middle * count, :]
        out_ref[:, (2 + k) * count : (3 + k) * count, :] = part.reshape(
            middle, count, rows
        ).astype(BF16)


def corr_kernel(*refs):
    in_ref, spec_ref = refs[:2]
    tabs = refs[2:8]
    out_ref, piece = refs[8:10]
    wide_ref, high_ref, low_ref, part_ref, grad_ref, back_ref, sem = refs[10:]
    blocks, two, rows = out_ref.shape
    count = two // 2
    middle = blocks // 2
    copy = pltpu.make_async_copy(in_ref.at[:, 3 * count :, :], piece, sem)
    copy.start()
    for k in range(2):
        part = in_ref[:, k * count : (k + 1) * count, :].astype(F32)
        wide_ref[k * middle * count : (k + 1) * middle * count, :] = part.reshape(-1, rows)

    def load(c):
        return wide_ref[pl.ds(c, blocks, stride=count), :]

    mine = (tabs[0].at[core()], *tabs[1:])
    forward(load, blocks, rows, count, mine, high_ref, low_ref, grad_ref)
    scale = 1.0 / (blocks * rows)
    for s, factor in ((1, scale), (0, scale / math.sqrt(blocks * rows))):

        def store(c, y):
            back_ref[1 - s, pl.ds(c, blocks, stride=count), :] = y

        product(spec_ref.at[s], grad_ref, True, high_ref, low_ref)
        inverse(high_ref, low_ref, part_ref, tabs, factor, blocks, rows, count, store)
    for k in range(2):
        out_ref[:, k * count : (k + 1) * count, :] = (
            back_ref[k].reshape(blocks, count, rows).astype(BF16)
        )
    copy.wait()


def weight_copies(w_hbm, chan, buf_ref, sem_ref):
    parts, band, width = buf_ref.shape
    columns = pl.ds(pl.multiple_of(chan * width, width), width)
    return [
        pltpu.make_async_copy(
            w_hbm.at[i * band : (i + 1) * band, columns], buf_ref.at[i], sem_ref.at[i]
        )
        for i in range(parts)
    ]


def project(gated_ref, buf_ref, copies, put):
    parts, band, width = buf_ref.shape
    total = 0.0
    for i in range(parts - 1):
        copies[i].wait()
        total = total + dot(gated_ref[:, i * band : (i + 1) * band], buf_ref[i])
    copies[-1].wait()
    step = width // 4
    for j in range(4):
        at = slice(j * step, (j + 1) * step)
        put(j, at, total[:, at] + dot(gated_ref[:, -band:], buf_ref[parts - 1, :, at]))


def mix_kernel(in_ref, *refs):
    other_ref, ss_ref, q_ref, w_hbm, send_hbm, gated_ref, mixing_ref = refs[:7]
    all_ref, buf_ref, send_ref, in_sem, out_sem = refs[7:]
    copies = weight_copies(w_hbm, 1 - lax.axis_index("chan"), buf_ref, in_sem)
    for copy in copies:
        copy.start()
    count = in_ref.shape[1] // 4
    all_ref[:, core()] = in_ref[:, 2 * count : 3 * count, :].astype(F32)
    all_ref[:, 1 - core()] = other_ref[...].astype(F32)
    mixing = all_ref[...].reshape(ss_ref.shape) + ss_ref[...]
    mixing_ref[...] = mixing
    gated_ref[...] = (mixing * q_ref[...].astype(F32)).T.astype(BF16)
    writes = []

    def put(j, at, product):
        send_ref[j] = product.astype(BF16)
        write = pltpu.make_async_copy(send_ref.at[j], send_hbm.at[:, at], out_sem.at[j])
        write.start()
        writes.append(write)

    project(gated_ref, buf_ref, copies, put)
    for write in writes:
        write.wait()


def own_kernel(
    mixing_ref, gg_ref, gated_ref, w_hbm, out_ref, gp_hbm, buf_ref, gq_ref, in_sem, out_sem
):
    copies = weight_copies(w_hbm, lax.axis_index("chan"), buf_ref, in_sem)
    for copy in copies:
        copy.start()
    gq_ref[...] = (mixing_ref[...] * gg_ref[...]).T.astype(BF16)
    write = pltpu.make_async_copy(gq_ref, gp_hbm.at[0], out_sem)
    write.start()

    def put(j, at, product):
        out_ref[:, at] = product

    project(gated_ref, buf_ref, copies, put)
    write.wait()


def end_kernel(in_ref, sg_ref, proj_ref, gp_in, gp_hbm, gf_hbm, gp_ref, gf_ref, sem_ref):
    parts, _, rows, width = gp_ref.shape
    step, count = in_ref.shape[0] // parts, in_ref.shape[1] // 2
    writes = []
    for i in range(parts):
        at = slice(i * width, (i + 1) * width)
        block = in_ref[i * step : (i + 1) * step].astype(F32)
        gf_ref[i] = block[:, count:].reshape(width, rows).T
        gs = block[:, :count].reshape(width, rows).T + sg_ref[:, at]
        gp_ref[i, 0] = (gs * proj_ref[2, :, at].astype(F32)).astype(BF16)
        gp_ref[i, 1] = (gs * proj_ref[1, :, at].astype(F32)).astype(BF16)
        for source, target in (
            (gf_ref.at[i], gf_hbm.at[:, at]),
            (gp_ref.at[i], gp_hbm.at[1:3, :, at]),
        ):
            write = pltpu.make_async_copy(source, target, sem_ref.at[len(writes)])
            write.start()
            writes.append(write)
    for write in writes:
        write.wait()


VMEM = pl.BlockSpec(memory_space=pltpu.VMEM)
HBM = pl.BlockSpec(memory_space=pltpu.HBM)


def conv_call(arrived, gm, tabs, each):
    blocks, _, rows = arrived.shape
    middle = blocks // 2
    spec_shape = (each * blocks, 2 * rows)
    return pl.pallas_call(
        conv_kernel,
        in_specs=[VMEM] + [HBM] * 2 + [VMEM] * len(tabs),
        out_specs=[VMEM] * 2,
        out_shape=[
            jax.ShapeDtypeStruct((2,) + spec_shape, F32),
            jax.ShapeDtypeStruct((middle, 4 * each, rows), BF16),
        ],
        scratch_shapes=[
            pltpu.VMEM((2, blocks * each, rows), F32),
            pltpu.VMEM(spec_shape, BF16),
            pltpu.VMEM(spec_shape, BF16),
            pltpu.VMEM(spec_shape, F32),
            pltpu.VMEM((blocks * each, rows), F32),
            pltpu.SemaphoreType.DMA((2,)),
        ],
        compiler_params=params(),
        name="conv",
    )(arrived, *gm, *tabs)


def corr_call(back, spectra, tabs, each):
    middle, _, rows = back.shape
    blocks = 2 * middle
    spec_shape = (each * blocks, 2 * rows)
    return pl.pallas_call(
        corr_kernel,
        in_specs=[VMEM] * (2 + len(tabs)),
        out_specs=[VMEM, HBM],
        out_shape=[jax.ShapeDtypeStruct((blocks, 2 * each, rows), BF16)]
        + [pltpu.HBM((middle, each, rows), BF16)],
        scratch_shapes=[
            pltpu.VMEM((blocks * each, rows), F32),
            pltpu.VMEM(spec_shape, BF16),
            pltpu.VMEM(spec_shape, BF16),
            pltpu.VMEM(spec_shape, F32),
            pltpu.VMEM(spec_shape, F32),
            pltpu.VMEM((2, blocks * each, rows), F32),
            pltpu.SemaphoreType.DMA(()),
        ],
        compiler_params=params(),
        cost_estimate=COSTLY,
        name="corr",
    )(back, spectra, *tabs)


def local(projected, skip_gain, out_weight, long_filter, cotangent):
    blocks = lax.axis_size("seq")
    rows, channels = long_filter.shape
    each = channels // blocks
    width = out_weight.shape[1]
    half = width // 2
    middle = blocks // 2
    tabs_conv, tabs_corr = tables(blocks, rows)
    chips = [[2 * m + near for m in range(middle)] for near in range(2)]

    def partner(x):
        return lax.ppermute(x, "seq", [(i, i ^ 1) for i in range(blocks)])

    in_hbm = lambda x: pltpu.with_memory_space_constraint(x, pltpu.HBM)
    proj = in_hbm(projected.transpose(1, 0, 2))
    out_weight = in_hbm(out_weight)
    long_filter = in_hbm(long_filter)
    skip = skip_gain.reshape(1, channels)
    full = lambda shape: pl.BlockSpec(shape, lambda *_: (0,) * len(shape))
    shape = jax.ShapeDtypeStruct

    other = lax.ppermute(cotangent, "chan", [(0, 1), (1, 0)])

    def exchange(x):
        return lax.all_to_all(x, "seq", 0, 0, tiled=True)

    vmem, hbm = VMEM, HBM
    parts = 4
    cb = channels // parts
    pb = blocks // parts
    fine = 2
    signals = pl.pallas_call(
        prep_kernel,
        in_specs=[hbm, hbm],
        out_specs=hbm,
        out_shape=shape((blocks, 2 * each, rows), BF16),
        scratch_shapes=[
            pltpu.VMEM((fine, 2, rows, channels // fine), BF16),
            pltpu.VMEM((fine, rows, channels // fine), F32),
            pltpu.VMEM((fine, blocks // fine, 2 * each, rows), BF16),
            pltpu.SemaphoreType.DMA((fine, 2)),
            pltpu.SemaphoreType.DMA((fine,)),
        ],
        compiler_params=params(),
        name="prep",
    )(proj, long_filter)
    arrived = exchange(signals)

    span = cb // (2 * each)
    query, gg, skip_source, skip_grad, gm_own, gm_give = pl.pallas_call(
        grad_kernel,
        grid_spec=pl.GridSpec(
            grid=(parts,),
            in_specs=[
                pl.BlockSpec((cb, width), lambda i: (i, 0)),
                full((rows, half)),
                full((rows, half)),
                pl.BlockSpec((3, rows, cb), lambda i: (0, 0, i)),
                pl.BlockSpec((1, cb), lambda i: (0, i)),
            ],
            out_specs=[pl.BlockSpec((cb, rows), lambda i: (i, 0))] * 3
            + [pl.BlockSpec((rows, cb), lambda i: (0, i))]
            + [hbm] * 2,
            scratch_shapes=[
                pltpu.VMEM((parts, 2, span, each, rows), BF16),
                pltpu.SemaphoreType.DMA((parts, 2)),
            ],
        ),
        out_shape=[shape((channels, rows), BF16)]
        + [shape((channels, rows), F32)] * 2
        + [shape((rows, channels), F32)]
        + [pltpu.HBM((middle, each, rows), BF16)] * 2,
        compiler_params=params(),
        cost_estimate=COSTLY,
        name="grad",
    )(out_weight, in_hbm(cotangent), in_hbm(other), proj, skip)
    gm = [in_hbm(gm_own), partner(gm_give)]

    spectra, mid = conv_call(arrived, gm, tabs_conv, each)
    back = lax.all_to_all(mid, "seq", 0, 0, tiled=True, axis_index_groups=chips)
    pair, conv_give = corr_call(back, spectra, tabs_corr, each)
    conv_got = partner(conv_give)
    last = exchange(pair)

    pieces = 4
    wb = half // pieces
    weights = pltpu.VMEM((pieces, channels // pieces, half), BF16)
    sems = pltpu.SemaphoreType.DMA((pieces,))
    send, gated, mixing = pl.pallas_call(
        mix_kernel,
        in_specs=[vmem] * 4 + [hbm],
        out_specs=[hbm, vmem, vmem],
        out_shape=[
            pltpu.HBM((rows, half), BF16),
            shape((rows, channels), BF16),
            shape((channels, rows), F32),
        ],
        scratch_shapes=[
            pltpu.VMEM((middle, 2, each, rows), F32),
            weights,
            pltpu.VMEM((pieces, rows, wb), BF16),
            sems,
            sems,
        ],
        compiler_params=params(),
        cost_estimate=COSTLY,
        name="mix",
    )(back, conv_got, skip_source, query, out_weight)
    received = lax.ppermute(send, "chan", [(0, 1), (1, 0)])
    kept, stacked = pl.pallas_call(
        own_kernel,
        in_specs=[vmem, vmem, vmem, hbm],
        out_specs=[vmem, hbm],
        out_shape=[shape((rows, half), F32), pltpu.HBM((3, rows, channels), BF16)],
        scratch_shapes=[
            weights,
            pltpu.VMEM((rows, channels), BF16),
            sems,
            pltpu.SemaphoreType.DMA(()),
        ],
        compiler_params=params(),
        name="own",
    )(mixing, in_hbm(gg), gated, out_weight)
    mixed = (kept + received.astype(F32)).astype(BF16)

    grad_projected, grad_filter = pl.pallas_call(
        end_kernel,
        in_specs=[vmem, vmem, vmem, hbm],
        out_specs=[hbm] * 2,
        out_shape=[shape((3, rows, channels), BF16), shape((rows, channels), F32)],
        scratch_shapes=[
            pltpu.VMEM((fine, 2, rows, channels // fine), BF16),
            pltpu.VMEM((fine, rows, channels // fine), F32),
            pltpu.SemaphoreType.DMA((2 * fine,)),
        ],
        input_output_aliases={3: 0},
        compiler_params=params(),
        name="end",
    )(last, skip_grad, projected.transpose(1, 0, 2), stacked)
    return mixed, grad_projected.transpose(1, 0, 2), grad_filter


def solution(mesh):
    in_specs = (
        P("seq", None, "chan"),
        P("chan"),
        P("chan", None),
        P("seq", "chan"),
        P("seq", "chan"),
    )
    out_specs = (P("seq", "chan"), P("seq", None, "chan"), P("seq", "chan"))
    return jax.shard_map(local, mesh=mesh, in_specs=in_specs, out_specs=out_specs, check_vma=False)
```

```python
import math

import jax
import jax.numpy as jnp
import numpy as np
from jax import lax
from jax.experimental import pallas as pl
from jax.experimental.pallas import tpu as pltpu
from jax.sharding import PartitionSpec as P

F32 = jnp.float32
BF16 = jnp.bfloat16
VMEM_LIMIT = 20 * 1024 * 1024
GAIN = 1.6657
COSTLY = pl.CostEstimate(flops=10**11, transcendentals=0, bytes_accessed=10**9)


def params():
    return pltpu.CompilerParams(vmem_limit_bytes=VMEM_LIMIT)


def halves(table):
    high = table.astype(BF16)
    low = (table - high.astype(np.float64)).astype(BF16)
    return high, low


def tables(blocks, rows):
    length = 2 * blocks * rows
    k1 = np.arange(blocks)[:, None] + 0.5
    angle = 2.0 * np.pi * k1 * np.arange(blocks)[None, :] / (2 * blocks)
    outer = np.concatenate([np.cos(angle), -np.sin(angle)], axis=0)
    outer_high, outer_low = halves(outer)
    outer_both = np.concatenate([outer_high, outer_low], axis=1)
    back = outer.T.astype(BF16)
    even = np.arange(blocks).reshape(blocks // 2, 2).T.reshape(-1)
    orders = [even, np.roll(even, blocks // 2)]
    outer_order = np.stack([np.concatenate([outer_high[:, o], outer_low[:, o]], 1) for o in orders])
    back_order = np.stack([outer.T[o].astype(BF16) for o in orders])
    turn = 2.0 * np.pi * k1 * np.arange(rows)[None, :] / length
    turn_re = np.cos(turn).astype(np.float32)
    turn_im = -np.sin(turn).astype(np.float32)
    grid = 2.0 * np.pi * (np.outer(np.arange(rows), np.arange(rows)) % rows) / rows
    cos, sin = np.cos(grid), np.sin(grid)
    inner = GAIN * np.block([[cos, -sin], [sin, cos]])
    shared = [turn_re, turn_im, inner.astype(BF16), inner.T.astype(BF16)]
    return [outer_both, back_order, *shared], [outer_order, back, *shared]


def dot(a, b):
    return jnp.dot(a, b, preferred_element_type=F32)


def transform(high_ref, low_ref, table):
    return dot(high_ref[...], table[...]) + dot(low_ref[...], table[...])


def dot_t(a, b):
    return lax.dot_general(a, b, (((1,), (1,)), ((), ())), preferred_element_type=F32)


def split(x):
    high = x.astype(BF16)
    return high, (x - high.astype(F32)).astype(BF16)


def forward(load, blocks, rows, count, tabs, high_ref, low_ref, spec_ref):
    outer, _, turn_re, turn_im, inner, _ = tabs
    tre, tim = turn_re[...], turn_im[...]
    for pair in range(count // 2):
        x = jnp.concatenate([load(2 * pair + j).astype(BF16) for j in range(2)], axis=1)
        a = dot(outer[...], jnp.concatenate([x, x], axis=0))
        for j in range(2):
            are = a[:blocks, j * rows : (j + 1) * rows]
            aim = a[blocks:, j * rows : (j + 1) * rows]
            b = jnp.concatenate([are * tre - aim * tim, are * tim + aim * tre], axis=1)
            high, low = split(b)
            at = (2 * pair + j) * blocks
            high_ref[at : at + blocks, :] = high
            low_ref[at : at + blocks, :] = low
    spec_ref[...] = transform(high_ref, low_ref, inner)


def inverse(high_ref, low_ref, part_ref, tabs, scale, blocks, rows, count, store):
    _, back, turn_re, turn_im, _, inner = tabs
    scale /= GAIN**3
    tre, tim = turn_re[...] * scale, turn_im[...] * scale
    part_ref[...] = transform(high_ref, low_ref, inner)
    for pair in range(count // 2):
        both = []
        for j in range(2):
            at = (2 * pair + j) * blocks
            cre = part_ref[at : at + blocks, :rows]
            cim = part_ref[at : at + blocks, rows:]
            both.append(jnp.concatenate([cre * tre + cim * tim, cim * tre - cre * tim], axis=0))
        high, low = split(jnp.concatenate(both, axis=1))
        y = dot(back[...], high) + dot(back[...], low)
        for j in range(2):
            store(2 * pair + j, y[:, j * rows : (j + 1) * rows])


def product(a_ref, b_ref, conj, high_ref, low_ref):
    half = a_ref.shape[1] // 2
    total = a_ref.shape[0]
    step = total // 8
    for i in range(8):
        at = slice(i * step, (i + 1) * step)
        ar, ai = a_ref[at, :half], a_ref[at, half:]
        br, bi = b_ref[at, :half], b_ref[at, half:]
        if conj:
            z = jnp.concatenate([ar * br + ai * bi, ar * bi - ai * br], axis=1)
        else:
            z = jnp.concatenate([ar * br - ai * bi, ar * bi + ai * br], axis=1)
        high, low = split(z)
        high_ref[at, :] = high
        low_ref[at, :] = low


def prep_kernel(proj_hbm, filter_hbm, out_hbm, pair_ref, filter_ref, out_ref, in_sem, out_sem):
    parts, _, rows, width = pair_ref.shape
    step, each = out_ref.shape[1], out_ref.shape[2] // 2
    reads, writes = [], []
    for i in range(parts):
        at = slice(i * width, (i + 1) * width)
        reads.append(
            (
                pltpu.make_async_copy(proj_hbm.at[1:3, :, at], pair_ref.at[i], in_sem.at[i, 0]),
                pltpu.make_async_copy(filter_hbm.at[:, at], filter_ref.at[i], in_sem.at[i, 1]),
            )
        )
        writes.append(
            pltpu.make_async_copy(
                out_ref.at[i], out_hbm.at[i * step : (i + 1) * step], out_sem.at[i]
            )
        )
    for pair, taps in reads:
        pair.start()
        taps.start()
    for i in range(parts):
        pair, taps = reads[i]
        pair.wait()
        source = pair_ref[i, 0].astype(F32) * pair_ref[i, 1].astype(F32)
        out_ref[i, :, :each, :] = source.T.reshape(step, each, rows).astype(BF16)
        taps.wait()
        out_ref[i, :, each:, :] = filter_ref[i].T.reshape(step, each, rows).astype(BF16)
        writes[i].start()
    for write in writes:
        write.wait()


def core():
    return lax.axis_index("seq") & 1


def grad_kernel(
    w_ref, own_ref, other_ref, proj_ref, skip_ref,
    q_ref, gg_ref, ss_ref, sg_ref, *rest,
):
    pieces, (gm_ref, sem_ref) = rest[:2], rest[2:]
    half = own_ref.shape[1]
    first = lax.axis_index("chan") == 0
    own, other = own_ref[...], other_ref[...]
    low = jnp.where(first, own, other)
    high = jnp.where(first, other, own)
    gg = dot_t(w_ref[:, :half], low) + dot_t(w_ref[:, half:], high)
    query = proj_ref[0].astype(F32).T
    gm = gg * query
    skip = skip_ref[...]
    gg_ref[...] = gg
    q_ref[...] = query.astype(BF16)
    step = pl.program_id(0)
    wide = gm.reshape(gm_ref.shape[2], 2, gm_ref.shape[3], gm.shape[1])
    for near in range(2):
        gm_ref[step, near] = wide[:, near].astype(BF16)
    sg_ref[...] = gm.T * skip
    ss_ref[...] = (proj_ref[1].astype(F32) * proj_ref[2].astype(F32) * skip).T
    steps, _, span = gm_ref.shape[:3]

    def copies(i, act):
        at = i * span
        for near in range(2):
            for k in range(2):

                @pl.when(near ^ core() == k)
                def _():
                    act(
                        pltpu.make_async_copy(
                            gm_ref.at[i, near], pieces[k].at[at : at + span], sem_ref.at[i, near]
                        )
                    )

    for i in range(steps):

        @pl.when(step == i)
        def _():
            copies(i, lambda copy: copy.start())

    @pl.when(step == steps - 1)
    def _():
        for i in range(steps):
            copies(i, lambda copy: copy.wait())


def conv_kernel(*refs):
    in_ref, gm_refs, tabs = refs[0], refs[1:3], refs[3:9]
    spec_ref, out_ref = refs[9:11]
    wide_ref, high_ref, low_ref, part_ref, back_ref, gm_sem = refs[11:]
    blocks, two, rows = in_ref.shape
    count = two // 2
    middle = blocks // 2
    copies = [
        pltpu.make_async_copy(
            gm_refs[k], out_ref.at[:, k * count : (k + 1) * count, :], gm_sem.at[k]
        )
        for k in range(2)
    ]
    for copy in copies:
        copy.start()
    for s in range(2):
        wide_ref[s] = in_ref[:, s * count : (s + 1) * count, :].astype(F32).reshape(-1, rows)

        def load(c):
            return wide_ref[s, pl.ds(c, blocks, stride=count), :]

        forward(load, blocks, rows, count, tabs, high_ref, low_ref, spec_ref.at[s])
    product(spec_ref.at[0], spec_ref.at[1], False, high_ref, low_ref)

    def store(c, y):
        back_ref[pl.ds(c, blocks, stride=count), :] = y

    mine = (tabs[0], tabs[1].at[core()], *tabs[2:])
    inverse(high_ref, low_ref, part_ref, mine, 1.0 / (blocks * rows), blocks, rows, count, store)
    for copy in copies:
        copy.wait()
    for k in range(2):
        part = back_ref[k * middle * count : (k + 1) * middle * count, :]
        out_ref[:, (2 + k) * count : (3 + k) * count, :] = part.reshape(
            middle, count, rows
        ).astype(BF16)


def corr_kernel(*refs):
    in_ref, spec_ref = refs[:2]
    tabs = refs[2:8]
    out_hbm, piece = refs[8:10]
    wide_ref, high_ref, low_ref, part_ref, grad_ref, back_ref, out_ref, sem, out_sem = refs[10:]
    blocks, two, rows = out_hbm.shape
    count = two // 2
    middle = blocks // 2
    copy = pltpu.make_async_copy(in_ref.at[:, 3 * count :, :], piece, sem)
    copy.start()
    for k in range(2):
        part = in_ref[:, k * count : (k + 1) * count, :].astype(F32)
        wide_ref[k * middle * count : (k + 1) * middle * count, :] = part.reshape(-1, rows)

    def load(c):
        return wide_ref[pl.ds(c, blocks, stride=count), :]

    mine = (tabs[0].at[core()], *tabs[1:])
    forward(load, blocks, rows, count, mine, high_ref, low_ref, grad_ref)
    scale = 1.0 / (blocks * rows)
    writes = []
    for s, factor in ((1, scale), (0, scale / math.sqrt(blocks * rows))):

        def store(c, y):
            back_ref[1 - s, pl.ds(c, blocks, stride=count), :] = y

        product(spec_ref.at[s], grad_ref, True, high_ref, low_ref)
        inverse(high_ref, low_ref, part_ref, tabs, factor, blocks, rows, count, store)
        k = 1 - s
        out_ref[k] = back_ref[k].reshape(blocks, count, rows).astype(BF16)
        writes.append(
            pltpu.make_async_copy(
                out_ref.at[k], out_hbm.at[:, k * count : (k + 1) * count, :], out_sem.at[k]
            )
        )
        writes[-1].start()
    for write in writes:
        write.wait()
    copy.wait()


def weight_copies(w_hbm, chan, buf_ref, sem_ref):
    parts, band, width = buf_ref.shape
    columns = pl.ds(pl.multiple_of(chan * width, width), width)
    part = band // 2
    return [
        pltpu.make_async_copy(
            w_hbm.at[i * band + j * part : i * band + (j + 1) * part, columns],
            buf_ref.at[i, j * part : (j + 1) * part],
            sem_ref.at[i, j],
        )
        for i in range(parts)
        for j in range(2)
    ]


def project(gated_ref, buf_ref, copies, put):
    parts, band, width = buf_ref.shape
    total = 0.0
    for i in range(parts - 1):
        copies[2 * i].wait()
        copies[2 * i + 1].wait()
        total = total + dot(gated_ref[:, i * band : (i + 1) * band], buf_ref[i])
    copies[-2].wait()
    copies[-1].wait()
    step = width // 4
    for j in range(4):
        at = slice(j * step, (j + 1) * step)
        put(j, at, total[:, at] + dot(gated_ref[:, -band:], buf_ref[parts - 1, :, at]))


def mix_kernel(in_ref, *refs):
    other_ref, ss_ref, q_ref, w_hbm, send_hbm, gated_ref, mixing_ref = refs[:7]
    all_ref, buf_ref, send_ref, in_sem, out_sem = refs[7:]
    copies = weight_copies(w_hbm, 1 - lax.axis_index("chan"), buf_ref, in_sem)
    for copy in copies:
        copy.start()
    count = in_ref.shape[1] // 4
    all_ref[:, core()] = in_ref[:, 2 * count : 3 * count, :].astype(F32)
    all_ref[:, 1 - core()] = other_ref[...].astype(F32)
    mixing = all_ref[...].reshape(ss_ref.shape) + ss_ref[...]
    mixing_ref[...] = mixing
    gated_ref[...] = (mixing * q_ref[...].astype(F32)).T.astype(BF16)
    writes = []

    def put(j, at, product):
        send_ref[j] = product.astype(BF16)
        write = pltpu.make_async_copy(send_ref.at[j], send_hbm.at[:, at], out_sem.at[j])
        write.start()
        writes.append(write)

    project(gated_ref, buf_ref, copies, put)
    for write in writes:
        write.wait()


def own_kernel(
    mixing_ref, gg_ref, gated_ref, w_hbm, out_ref, gp_hbm, buf_ref, gq_ref, in_sem, out_sem
):
    copies = weight_copies(w_hbm, lax.axis_index("chan"), buf_ref, in_sem)
    for copy in copies:
        copy.start()
    gq_ref[...] = (mixing_ref[...] * gg_ref[...]).T.astype(BF16)
    write = pltpu.make_async_copy(gq_ref, gp_hbm.at[0], out_sem)
    write.start()

    def put(j, at, product):
        out_ref[:, at] = product

    project(gated_ref, buf_ref, copies, put)
    write.wait()


def end_kernel(in_ref, sg_ref, proj_ref, gp_in, gp_hbm, gf_hbm, gp_ref, gf_ref, sem_ref):
    parts, _, rows, width = gp_ref.shape
    step, count = in_ref.shape[0] // parts, in_ref.shape[1] // 2
    writes = []
    for i in range(parts):
        at = slice(i * width, (i + 1) * width)
        block = in_ref[i * step : (i + 1) * step].astype(F32)
        gf_ref[i] = block[:, count:].reshape(width, rows).T
        gs = block[:, :count].reshape(width, rows).T + sg_ref[:, at]
        gp_ref[i, 0] = (gs * proj_ref[2, :, at].astype(F32)).astype(BF16)
        gp_ref[i, 1] = (gs * proj_ref[1, :, at].astype(F32)).astype(BF16)
        for source, target in (
            (gf_ref.at[i], gf_hbm.at[:, at]),
            (gp_ref.at[i], gp_hbm.at[1:3, :, at]),
        ):
            write = pltpu.make_async_copy(source, target, sem_ref.at[len(writes)])
            write.start()
            writes.append(write)
    for write in writes:
        write.wait()


VMEM = pl.BlockSpec(memory_space=pltpu.VMEM)
HBM = pl.BlockSpec(memory_space=pltpu.HBM)


def conv_call(arrived, gm, tabs, each):
    blocks, _, rows = arrived.shape
    middle = blocks // 2
    spec_shape = (each * blocks, 2 * rows)
    return pl.pallas_call(
        conv_kernel,
        in_specs=[VMEM] + [HBM] * 2 + [VMEM] * len(tabs),
        out_specs=[VMEM] * 2,
        out_shape=[
            jax.ShapeDtypeStruct((2,) + spec_shape, F32),
            jax.ShapeDtypeStruct((middle, 4 * each, rows), BF16),
        ],
        scratch_shapes=[
            pltpu.VMEM((2, blocks * each, rows), F32),
            pltpu.VMEM(spec_shape, BF16),
            pltpu.VMEM(spec_shape, BF16),
            pltpu.VMEM(spec_shape, F32),
            pltpu.VMEM((blocks * each, rows), F32),
            pltpu.SemaphoreType.DMA((2,)),
        ],
        compiler_params=params(),
        name="conv",
    )(arrived, *gm, *tabs)


def corr_call(back, spectra, tabs, each):
    middle, _, rows = back.shape
    blocks = 2 * middle
    spec_shape = (each * blocks, 2 * rows)
    return pl.pallas_call(
        corr_kernel,
        in_specs=[VMEM] * (2 + len(tabs)),
        out_specs=[HBM, HBM],
        out_shape=[pltpu.HBM((blocks, 2 * each, rows), BF16)]
        + [pltpu.HBM((middle, each, rows), BF16)],
        scratch_shapes=[
            pltpu.VMEM((blocks * each, rows), F32),
            pltpu.VMEM(spec_shape, BF16),
            pltpu.VMEM(spec_shape, BF16),
            pltpu.VMEM(spec_shape, F32),
            pltpu.VMEM(spec_shape, F32),
            pltpu.VMEM((2, blocks * each, rows), F32),
            pltpu.VMEM((2, blocks, each, rows), BF16),
            pltpu.SemaphoreType.DMA(()),
            pltpu.SemaphoreType.DMA((2,)),
        ],
        compiler_params=params(),
        cost_estimate=COSTLY,
        name="corr",
    )(back, spectra, *tabs)


def local(projected, skip_gain, out_weight, long_filter, cotangent):
    blocks = lax.axis_size("seq")
    rows, channels = long_filter.shape
    each = channels // blocks
    width = out_weight.shape[1]
    half = width // 2
    middle = blocks // 2
    tabs_conv, tabs_corr = tables(blocks, rows)
    chips = [[2 * m + near for m in range(middle)] for near in range(2)]

    def partner(x):
        return lax.ppermute(x, "seq", [(i, i ^ 1) for i in range(blocks)])

    in_hbm = lambda x: pltpu.with_memory_space_constraint(x, pltpu.HBM)
    proj = in_hbm(projected.transpose(1, 0, 2))
    out_weight = in_hbm(out_weight)
    long_filter = in_hbm(long_filter)
    skip = skip_gain.reshape(1, channels)
    full = lambda shape: pl.BlockSpec(shape, lambda *_: (0,) * len(shape))
    shape = jax.ShapeDtypeStruct

    other = lax.ppermute(cotangent, "chan", [(0, 1), (1, 0)])

    def exchange(x):
        return lax.all_to_all(x, "seq", 0, 0, tiled=True)

    vmem, hbm = VMEM, HBM
    parts = 4
    cb = channels // parts
    pb = blocks // parts
    fine = 2
    signals = pl.pallas_call(
        prep_kernel,
        in_specs=[hbm, hbm],
        out_specs=hbm,
        out_shape=shape((blocks, 2 * each, rows), BF16),
        scratch_shapes=[
            pltpu.VMEM((fine, 2, rows, channels // fine), BF16),
            pltpu.VMEM((fine, rows, channels // fine), F32),
            pltpu.VMEM((fine, blocks // fine, 2 * each, rows), BF16),
            pltpu.SemaphoreType.DMA((fine, 2)),
            pltpu.SemaphoreType.DMA((fine,)),
        ],
        compiler_params=params(),
        name="prep",
    )(proj, long_filter)
    arrived = exchange(signals)

    span = cb // (2 * each)
    query, gg, skip_source, skip_grad, gm_own, gm_give = pl.pallas_call(
        grad_kernel,
        grid_spec=pl.GridSpec(
            grid=(parts,),
            in_specs=[
                pl.BlockSpec((cb, width), lambda i: (i, 0)),
                full((rows, half)),
                full((rows, half)),
                pl.BlockSpec((3, rows, cb), lambda i: (0, 0, i)),
                pl.BlockSpec((1, cb), lambda i: (0, i)),
            ],
            out_specs=[pl.BlockSpec((cb, rows), lambda i: (i, 0))] * 3
            + [pl.BlockSpec((rows, cb), lambda i: (0, i))]
            + [hbm] * 2,
            scratch_shapes=[
                pltpu.VMEM((parts, 2, span, each, rows), BF16),
                pltpu.SemaphoreType.DMA((parts, 2)),
            ],
        ),
        out_shape=[shape((channels, rows), BF16)]
        + [shape((channels, rows), F32)] * 2
        + [shape((rows, channels), F32)]
        + [pltpu.HBM((middle, each, rows), BF16)] * 2,
        compiler_params=params(),
        cost_estimate=COSTLY,
        name="grad",
    )(out_weight, in_hbm(cotangent), in_hbm(other), proj, skip)
    gm = [in_hbm(gm_own), partner(gm_give)]

    spectra, mid = conv_call(arrived, gm, tabs_conv, each)
    back = lax.all_to_all(mid, "seq", 0, 0, tiled=True, axis_index_groups=chips)
    pair, conv_give = corr_call(back, spectra, tabs_corr, each)
    conv_got = partner(conv_give)
    last = exchange(pair)

    pieces = 4
    wb = half // pieces
    weights = pltpu.VMEM((pieces, channels // pieces, half), BF16)
    sems = pltpu.SemaphoreType.DMA((pieces, 2))
    send, gated, mixing = pl.pallas_call(
        mix_kernel,
        in_specs=[vmem] * 4 + [hbm],
        out_specs=[hbm, vmem, vmem],
        out_shape=[
            pltpu.HBM((rows, half), BF16),
            shape((rows, channels), BF16),
            shape((channels, rows), F32),
        ],
        scratch_shapes=[
            pltpu.VMEM((middle, 2, each, rows), F32),
            weights,
            pltpu.VMEM((pieces, rows, wb), BF16),
            sems,
            pltpu.SemaphoreType.DMA((pieces,)),
        ],
        compiler_params=params(),
        cost_estimate=COSTLY,
        name="mix",
    )(back, conv_got, skip_source, query, out_weight)
    received = lax.ppermute(send, "chan", [(0, 1), (1, 0)])
    kept, stacked = pl.pallas_call(
        own_kernel,
        in_specs=[vmem, vmem, vmem, hbm],
        out_specs=[vmem, hbm],
        out_shape=[shape((rows, half), F32), pltpu.HBM((3, rows, channels), BF16)],
        scratch_shapes=[
            weights,
            pltpu.VMEM((rows, channels), BF16),
            sems,
            pltpu.SemaphoreType.DMA(()),
        ],
        compiler_params=params(),
        name="own",
    )(mixing, in_hbm(gg), gated, out_weight)
    mixed = (kept + received.astype(F32)).astype(BF16)

    grad_projected, grad_filter = pl.pallas_call(
        end_kernel,
        in_specs=[vmem, vmem, vmem, hbm],
        out_specs=[hbm] * 2,
        out_shape=[shape((3, rows, channels), BF16), shape((rows, channels), F32)],
        scratch_shapes=[
            pltpu.VMEM((fine, 2, rows, channels // fine), BF16),
            pltpu.VMEM((fine, rows, channels // fine), F32),
            pltpu.SemaphoreType.DMA((2 * fine,)),
        ],
        input_output_aliases={3: 0},
        compiler_params=params(),
        name="end",
    )(last, skip_grad, projected.transpose(1, 0, 2), stacked)
    return mixed, grad_projected.transpose(1, 0, 2), grad_filter


def solution(mesh):
    in_specs = (
        P("seq", None, "chan"),
        P("chan"),
        P("chan", None),
        P("seq", "chan"),
        P("seq", "chan"),
    )
    out_specs = (P("seq", "chan"), P("seq", None, "chan"), P("seq", "chan"))
    return jax.shard_map(local, mesh=mesh, in_specs=in_specs, out_specs=out_specs, check_vma=False)
```

```python
import math

import jax
import jax.numpy as jnp
import numpy as np
from jax import lax
from jax.experimental import pallas as pl
from jax.experimental.pallas import tpu as pltpu
from jax.sharding import PartitionSpec as P

F32 = jnp.float32
BF16 = jnp.bfloat16
VMEM_LIMIT = 20 * 1024 * 1024
GAIN = 1.6657
COSTLY = pl.CostEstimate(flops=10**11, transcendentals=0, bytes_accessed=10**9)


def params():
    return pltpu.CompilerParams(vmem_limit_bytes=VMEM_LIMIT)


def halves(table):
    high = table.astype(BF16)
    low = (table - high.astype(np.float64)).astype(BF16)
    return high, low


def tables(blocks, rows):
    length = 2 * blocks * rows
    k1 = np.arange(blocks)[:, None] + 0.5
    angle = 2.0 * np.pi * k1 * np.arange(blocks)[None, :] / (2 * blocks)
    outer = np.concatenate([np.cos(angle), -np.sin(angle)], axis=0)
    back = outer.T.astype(BF16)
    even = np.arange(blocks).reshape(blocks // 2, 2).T.reshape(-1)
    orders = [even, np.roll(even, blocks // 2)]
    outer_order = np.stack([outer[:, o].astype(BF16) for o in orders])
    back_order = np.stack([outer.T[o].astype(BF16) for o in orders])
    turn = 2.0 * np.pi * k1 * np.arange(rows)[None, :] / length
    turn_re = np.cos(turn).astype(np.float32)
    turn_im = -np.sin(turn).astype(np.float32)
    grid = 2.0 * np.pi * (np.outer(np.arange(rows), np.arange(rows)) % rows) / rows
    cos, sin = np.cos(grid), np.sin(grid)
    inner = GAIN * np.block([[cos, -sin], [sin, cos]])
    shared = [turn_re, turn_im, inner.astype(BF16), inner.T.astype(BF16)]
    return [outer.astype(BF16), back_order, *shared], [outer_order, back, *shared]


def dot(a, b):
    return jnp.dot(a, b, preferred_element_type=F32)


def transform(high_ref, low_ref, table):
    return dot(high_ref[...], table[...]) + dot(low_ref[...], table[...])


def dot_t(a, b):
    return lax.dot_general(a, b, (((1,), (1,)), ((), ())), preferred_element_type=F32)


def split(x):
    high = x.astype(BF16)
    return high, (x - high.astype(F32)).astype(BF16)


def forward(load, blocks, rows, count, tabs, high_ref, low_ref, spec_ref):
    outer, _, turn_re, turn_im, inner, _ = tabs
    tre, tim = turn_re[...], turn_im[...]
    for pair in range(count // 2):
        x = jnp.concatenate([load(2 * pair + j).astype(BF16) for j in range(2)], axis=1)
        a = dot(outer[...], x)
        for j in range(2):
            are = a[:blocks, j * rows : (j + 1) * rows]
            aim = a[blocks:, j * rows : (j + 1) * rows]
            b = jnp.concatenate([are * tre - aim * tim, are * tim + aim * tre], axis=1)
            high, low = split(b)
            at = (2 * pair + j) * blocks
            high_ref[at : at + blocks, :] = high
            low_ref[at : at + blocks, :] = low
    spec_ref[...] = transform(high_ref, low_ref, inner)


def inverse(high_ref, low_ref, part_ref, tabs, scale, blocks, rows, count, store):
    _, back, turn_re, turn_im, _, inner = tabs
    scale /= GAIN**3
    tre, tim = turn_re[...] * scale, turn_im[...] * scale
    part_ref[...] = transform(high_ref, low_ref, inner)
    for pair in range(count // 2):
        both = []
        for j in range(2):
            at = (2 * pair + j) * blocks
            cre = part_ref[at : at + blocks, :rows]
            cim = part_ref[at : at + blocks, rows:]
            both.append(jnp.concatenate([cre * tre + cim * tim, cim * tre - cre * tim], axis=0))
        high, low = split(jnp.concatenate(both, axis=1))
        y = dot(back[...], high) + dot(back[...], low)
        for j in range(2):
            store(2 * pair + j, y[:, j * rows : (j + 1) * rows])


def product(a_ref, b_ref, conj, high_ref, low_ref):
    half = a_ref.shape[1] // 2
    total = a_ref.shape[0]
    step = total // 8
    for i in range(8):
        at = slice(i * step, (i + 1) * step)
        ar, ai = a_ref[at, :half], a_ref[at, half:]
        br, bi = b_ref[at, :half], b_ref[at, half:]
        if conj:
            z = jnp.concatenate([ar * br + ai * bi, ar * bi - ai * br], axis=1)
        else:
            z = jnp.concatenate([ar * br - ai * bi, ar * bi + ai * br], axis=1)
        high, low = split(z)
        high_ref[at, :] = high
        low_ref[at, :] = low


def prep_kernel(proj_hbm, filter_hbm, out_hbm, pair_ref, filter_ref, out_ref, in_sem, out_sem):
    parts, _, rows, width = pair_ref.shape
    step, each = out_ref.shape[1], out_ref.shape[2] // 2
    reads, writes = [], []
    for i in range(parts):
        at = slice(i * width, (i + 1) * width)
        reads.append(
            (
                pltpu.make_async_copy(proj_hbm.at[1:3, :, at], pair_ref.at[i], in_sem.at[i, 0]),
                pltpu.make_async_copy(filter_hbm.at[:, at], filter_ref.at[i], in_sem.at[i, 1]),
            )
        )
        writes.append(
            pltpu.make_async_copy(
                out_ref.at[i], out_hbm.at[i * step : (i + 1) * step], out_sem.at[i]
            )
        )
    for pair, taps in reads:
        pair.start()
        taps.start()
    for i in range(parts):
        pair, taps = reads[i]
        pair.wait()
        source = pair_ref[i, 0].astype(F32) * pair_ref[i, 1].astype(F32)
        out_ref[i, :, :each, :] = source.T.reshape(step, each, rows).astype(BF16)
        taps.wait()
        out_ref[i, :, each:, :] = filter_ref[i].T.reshape(step, each, rows).astype(BF16)
        writes[i].start()
    for write in writes:
        write.wait()


def core():
    return lax.axis_index("seq") & 1


def grad_kernel(
    w_ref, own_ref, other_ref, proj_ref, skip_ref,
    q_ref, gg_ref, ss_ref, sg_ref, *rest,
):
    pieces, (gm_ref, sem_ref) = rest[:2], rest[2:]
    half = own_ref.shape[1]
    first = lax.axis_index("chan") == 0
    own, other = own_ref[...], other_ref[...]
    low = jnp.where(first, own, other)
    high = jnp.where(first, other, own)
    gg = dot_t(w_ref[:, :half], low) + dot_t(w_ref[:, half:], high)
    query = proj_ref[0].astype(F32).T
    gm = gg * query
    skip = skip_ref[...]
    gg_ref[...] = gg
    q_ref[...] = query.astype(BF16)
    step = pl.program_id(0)
    wide = gm.reshape(gm_ref.shape[2], 2, gm_ref.shape[3], gm.shape[1])
    for near in range(2):
        gm_ref[step, near] = wide[:, near].astype(BF16)
    sg_ref[...] = gm.T * skip
    ss_ref[...] = (proj_ref[1].astype(F32) * proj_ref[2].astype(F32) * skip).T
    steps, _, span = gm_ref.shape[:3]

    def copies(i, act):
        at = i * span
        for near in range(2):
            for k in range(2):

                @pl.when(near ^ core() == k)
                def _():
                    act(
                        pltpu.make_async_copy(
                            gm_ref.at[i, near], pieces[k].at[at : at + span], sem_ref.at[i, near]
                        )
                    )

    for i in range(steps):

        @pl.when(step == i)
        def _():
            copies(i, lambda copy: copy.start())

    @pl.when(step == steps - 1)
    def _():
        for i in range(steps):
            copies(i, lambda copy: copy.wait())


def conv_kernel(*refs):
    in_ref, gm_refs, tabs = refs[0], refs[1:3], refs[3:9]
    spec_ref, out_ref = refs[9:11]
    wide_ref, high_ref, low_ref, part_ref, back_ref, gm_sem = refs[11:]
    blocks, two, rows = in_ref.shape
    count = two // 2
    middle = blocks // 2
    copies = [
        pltpu.make_async_copy(
            gm_refs[k], out_ref.at[:, k * count : (k + 1) * count, :], gm_sem.at[k]
        )
        for k in range(2)
    ]
    for copy in copies:
        copy.start()
    for s in range(2):
        wide_ref[s] = in_ref[:, s * count : (s + 1) * count, :].astype(F32).reshape(-1, rows)

        def load(c):
            return wide_ref[s, pl.ds(c, blocks, stride=count), :]

        forward(load, blocks, rows, count, tabs, high_ref, low_ref, spec_ref.at[s])
    product(spec_ref.at[0], spec_ref.at[1], False, high_ref, low_ref)

    def store(c, y):
        back_ref[pl.ds(c, blocks, stride=count), :] = y

    mine = (tabs[0], tabs[1].at[core()], *tabs[2:])
    inverse(high_ref, low_ref, part_ref, mine, 1.0 / (blocks * rows), blocks, rows, count, store)
    for copy in copies:
        copy.wait()
    for k in range(2):
        part = back_ref[k * middle * count : (k + 1) * middle * count, :]
        out_ref[:, (2 + k) * count : (3 + k) * count, :] = part.reshape(
            middle, count, rows
        ).astype(BF16)


def corr_kernel(*refs):
    in_ref, spec_ref = refs[:2]
    tabs = refs[2:8]
    out_hbm, piece = refs[8:10]
    wide_ref, high_ref, low_ref, part_ref, grad_ref, back_ref, out_ref, sem, out_sem = refs[10:]
    blocks, two, rows = out_hbm.shape
    count = two // 2
    middle = blocks // 2
    copy = pltpu.make_async_copy(in_ref.at[:, 3 * count :, :], piece, sem)
    copy.start()
    for k in range(2):
        part = in_ref[:, k * count : (k + 1) * count, :].astype(F32)
        wide_ref[k * middle * count : (k + 1) * middle * count, :] = part.reshape(-1, rows)

    def load(c):
        return wide_ref[pl.ds(c, blocks, stride=count), :]

    mine = (tabs[0].at[core()], *tabs[1:])
    forward(load, blocks, rows, count, mine, high_ref, low_ref, grad_ref)
    scale = 1.0 / (blocks * rows)
    writes = []
    for s, factor in ((1, scale), (0, scale / math.sqrt(blocks * rows))):

        def store(c, y):
            back_ref[1 - s, pl.ds(c, blocks, stride=count), :] = y

        product(spec_ref.at[s], grad_ref, True, high_ref, low_ref)
        inverse(high_ref, low_ref, part_ref, tabs, factor, blocks, rows, count, store)
        k = 1 - s
        out_ref[k] = back_ref[k].reshape(blocks, count, rows).astype(BF16)
        writes.append(
            pltpu.make_async_copy(
                out_ref.at[k], out_hbm.at[:, k * count : (k + 1) * count, :], out_sem.at[k]
            )
        )
        writes[-1].start()
    for write in writes:
        write.wait()
    copy.wait()


def weight_copies(w_hbm, chan, buf_ref, sem_ref):
    parts, band, width = buf_ref.shape
    columns = pl.ds(pl.multiple_of(chan * width, width), width)
    part = band // 2
    return [
        pltpu.make_async_copy(
            w_hbm.at[i * band + j * part : i * band + (j + 1) * part, columns],
            buf_ref.at[i, j * part : (j + 1) * part],
            sem_ref.at[i, j],
        )
        for i in range(parts)
        for j in range(2)
    ]


def project(gated_ref, buf_ref, copies, put):
    parts, band, width = buf_ref.shape
    total = 0.0
    for i in range(parts - 1):
        copies[2 * i].wait()
        copies[2 * i + 1].wait()
        total = total + dot(gated_ref[:, i * band : (i + 1) * band], buf_ref[i])
    copies[-2].wait()
    copies[-1].wait()
    step = width // 4
    for j in range(4):
        at = slice(j * step, (j + 1) * step)
        put(j, at, total[:, at] + dot(gated_ref[:, -band:], buf_ref[parts - 1, :, at]))


def mix_kernel(in_ref, *refs):
    other_ref, ss_ref, q_ref, w_hbm, send_hbm, gated_ref, mixing_ref = refs[:7]
    all_ref, buf_ref, send_ref, in_sem, out_sem = refs[7:]
    copies = weight_copies(w_hbm, 1 - lax.axis_index("chan"), buf_ref, in_sem)
    for copy in copies:
        copy.start()
    count = in_ref.shape[1] // 4
    all_ref[:, core()] = in_ref[:, 2 * count : 3 * count, :].astype(F32)
    all_ref[:, 1 - core()] = other_ref[...].astype(F32)
    mixing = all_ref[...].reshape(ss_ref.shape) + ss_ref[...]
    mixing_ref[...] = mixing
    gated_ref[...] = (mixing * q_ref[...].astype(F32)).T.astype(BF16)
    writes = []

    def put(j, at, product):
        send_ref[j] = product.astype(BF16)
        write = pltpu.make_async_copy(send_ref.at[j], send_hbm.at[:, at], out_sem.at[j])
        write.start()
        writes.append(write)

    project(gated_ref, buf_ref, copies, put)
    for write in writes:
        write.wait()


def own_kernel(
    mixing_ref, gg_ref, gated_ref, w_hbm, out_ref, gp_hbm, buf_ref, gq_ref, in_sem, out_sem
):
    copies = weight_copies(w_hbm, lax.axis_index("chan"), buf_ref, in_sem)
    for copy in copies:
        copy.start()
    gq_ref[...] = (mixing_ref[...] * gg_ref[...]).T.astype(BF16)
    write = pltpu.make_async_copy(gq_ref, gp_hbm.at[0], out_sem)
    write.start()

    def put(j, at, product):
        out_ref[:, at] = product

    project(gated_ref, buf_ref, copies, put)
    write.wait()


def end_kernel(in_ref, sg_ref, proj_ref, gp_in, gp_hbm, gf_hbm, gp_ref, gf_ref, sem_ref):
    parts, _, rows, width = gp_ref.shape
    step, count = in_ref.shape[0] // parts, in_ref.shape[1] // 2
    writes = []
    for i in range(parts):
        at = slice(i * width, (i + 1) * width)
        block = in_ref[i * step : (i + 1) * step].astype(F32)
        gf_ref[i] = block[:, count:].reshape(width, rows).T
        gs = block[:, :count].reshape(width, rows).T + sg_ref[:, at]
        gp_ref[i, 0] = (gs * proj_ref[2, :, at].astype(F32)).astype(BF16)
        gp_ref[i, 1] = (gs * proj_ref[1, :, at].astype(F32)).astype(BF16)
        for source, target in (
            (gf_ref.at[i], gf_hbm.at[:, at]),
            (gp_ref.at[i], gp_hbm.at[1:3, :, at]),
        ):
            write = pltpu.make_async_copy(source, target, sem_ref.at[len(writes)])
            write.start()
            writes.append(write)
    for write in writes:
        write.wait()


VMEM = pl.BlockSpec(memory_space=pltpu.VMEM)
HBM = pl.BlockSpec(memory_space=pltpu.HBM)


def conv_call(arrived, gm, tabs, each):
    blocks, _, rows = arrived.shape
    middle = blocks // 2
    spec_shape = (each * blocks, 2 * rows)
    return pl.pallas_call(
        conv_kernel,
        in_specs=[VMEM] + [HBM] * 2 + [VMEM] * len(tabs),
        out_specs=[VMEM] * 2,
        out_shape=[
            jax.ShapeDtypeStruct((2,) + spec_shape, F32),
            jax.ShapeDtypeStruct((middle, 4 * each, rows), BF16),
        ],
        scratch_shapes=[
            pltpu.VMEM((2, blocks * each, rows), F32),
            pltpu.VMEM(spec_shape, BF16),
            pltpu.VMEM(spec_shape, BF16),
            pltpu.VMEM(spec_shape, F32),
            pltpu.VMEM((blocks * each, rows), F32),
            pltpu.SemaphoreType.DMA((2,)),
        ],
        compiler_params=params(),
        name="conv",
    )(arrived, *gm, *tabs)


def corr_call(back, spectra, tabs, each):
    middle, _, rows = back.shape
    blocks = 2 * middle
    spec_shape = (each * blocks, 2 * rows)
    return pl.pallas_call(
        corr_kernel,
        in_specs=[VMEM] * (2 + len(tabs)),
        out_specs=[HBM, HBM],
        out_shape=[pltpu.HBM((blocks, 2 * each, rows), BF16)]
        + [pltpu.HBM((middle, each, rows), BF16)],
        scratch_shapes=[
            pltpu.VMEM((blocks * each, rows), F32),
            pltpu.VMEM(spec_shape, BF16),
            pltpu.VMEM(spec_shape, BF16),
            pltpu.VMEM(spec_shape, F32),
            pltpu.VMEM(spec_shape, F32),
            pltpu.VMEM((2, blocks * each, rows), F32),
            pltpu.VMEM((2, blocks, each, rows), BF16),
            pltpu.SemaphoreType.DMA(()),
            pltpu.SemaphoreType.DMA((2,)),
        ],
        compiler_params=params(),
        cost_estimate=COSTLY,
        name="corr",
    )(back, spectra, *tabs)


def local(projected, skip_gain, out_weight, long_filter, cotangent):
    blocks = lax.axis_size("seq")
    rows, channels = long_filter.shape
    each = channels // blocks
    width = out_weight.shape[1]
    half = width // 2
    middle = blocks // 2
    tabs_conv, tabs_corr = tables(blocks, rows)
    chips = [[2 * m + near for m in range(middle)] for near in range(2)]

    def partner(x):
        return lax.ppermute(x, "seq", [(i, i ^ 1) for i in range(blocks)])

    in_hbm = lambda x: pltpu.with_memory_space_constraint(x, pltpu.HBM)
    proj = in_hbm(projected.transpose(1, 0, 2))
    out_weight = in_hbm(out_weight)
    long_filter = in_hbm(long_filter)
    skip = skip_gain.reshape(1, channels)
    full = lambda shape: pl.BlockSpec(shape, lambda *_: (0,) * len(shape))
    shape = jax.ShapeDtypeStruct

    other = lax.ppermute(cotangent, "chan", [(0, 1), (1, 0)])

    def exchange(x):
        return lax.all_to_all(x, "seq", 0, 0, tiled=True)

    vmem, hbm = VMEM, HBM
    parts = 4
    cb = channels // parts
    pb = blocks // parts
    fine = 2
    signals = pl.pallas_call(
        prep_kernel,
        in_specs=[hbm, hbm],
        out_specs=hbm,
        out_shape=shape((blocks, 2 * each, rows), BF16),
        scratch_shapes=[
            pltpu.VMEM((fine, 2, rows, channels // fine), BF16),
            pltpu.VMEM((fine, rows, channels // fine), F32),
            pltpu.VMEM((fine, blocks // fine, 2 * each, rows), BF16),
            pltpu.SemaphoreType.DMA((fine, 2)),
            pltpu.SemaphoreType.DMA((fine,)),
        ],
        compiler_params=params(),
        name="prep",
    )(proj, long_filter)
    arrived = exchange(signals)

    span = cb // (2 * each)
    query, gg, skip_source, skip_grad, gm_own, gm_give = pl.pallas_call(
        grad_kernel,
        grid_spec=pl.GridSpec(
            grid=(parts,),
            in_specs=[
                pl.BlockSpec((cb, width), lambda i: (i, 0)),
                full((rows, half)),
                full((rows, half)),
                pl.BlockSpec((3, rows, cb), lambda i: (0, 0, i)),
                pl.BlockSpec((1, cb), lambda i: (0, i)),
            ],
            out_specs=[pl.BlockSpec((cb, rows), lambda i: (i, 0))] * 3
            + [pl.BlockSpec((rows, cb), lambda i: (0, i))]
            + [hbm] * 2,
            scratch_shapes=[
                pltpu.VMEM((parts, 2, span, each, rows), BF16),
                pltpu.SemaphoreType.DMA((parts, 2)),
            ],
        ),
        out_shape=[shape((channels, rows), BF16)]
        + [shape((channels, rows), F32)] * 2
        + [shape((rows, channels), F32)]
        + [pltpu.HBM((middle, each, rows), BF16)] * 2,
        compiler_params=params(),
        cost_estimate=COSTLY,
        name="grad",
    )(out_weight, in_hbm(cotangent), in_hbm(other), proj, skip)
    gm = [in_hbm(gm_own), partner(gm_give)]

    spectra, mid = conv_call(arrived, gm, tabs_conv, each)
    back = lax.all_to_all(mid, "seq", 0, 0, tiled=True, axis_index_groups=chips)
    pair, conv_give = corr_call(back, spectra, tabs_corr, each)
    conv_got = partner(conv_give)
    last = exchange(pair)

    pieces = 4
    wb = half // pieces
    weights = pltpu.VMEM((pieces, channels // pieces, half), BF16)
    sems = pltpu.SemaphoreType.DMA((pieces, 2))
    send, gated, mixing = pl.pallas_call(
        mix_kernel,
        in_specs=[vmem] * 4 + [hbm],
        out_specs=[hbm, vmem, vmem],
        out_shape=[
            pltpu.HBM((rows, half), BF16),
            shape((rows, channels), BF16),
            shape((channels, rows), F32),
        ],
        scratch_shapes=[
            pltpu.VMEM((middle, 2, each, rows), F32),
            weights,
            pltpu.VMEM((pieces, rows, wb), BF16),
            sems,
            pltpu.SemaphoreType.DMA((pieces,)),
        ],
        compiler_params=params(),
        cost_estimate=COSTLY,
        name="mix",
    )(back, conv_got, skip_source, query, out_weight)
    received = lax.ppermute(send, "chan", [(0, 1), (1, 0)])
    kept, stacked = pl.pallas_call(
        own_kernel,
        in_specs=[vmem, vmem, vmem, hbm],
        out_specs=[vmem, hbm],
        out_shape=[shape((rows, half), F32), pltpu.HBM((3, rows, channels), BF16)],
        scratch_shapes=[
            weights,
            pltpu.VMEM((rows, channels), BF16),
            sems,
            pltpu.SemaphoreType.DMA(()),
        ],
        compiler_params=params(),
        name="own",
    )(mixing, in_hbm(gg), gated, out_weight)
    mixed = (kept + received.astype(F32)).astype(BF16)

    grad_projected, grad_filter = pl.pallas_call(
        end_kernel,
        in_specs=[vmem, vmem, vmem, hbm],
        out_specs=[hbm] * 2,
        out_shape=[shape((3, rows, channels), BF16), shape((rows, channels), F32)],
        scratch_shapes=[
            pltpu.VMEM((fine, 2, rows, channels // fine), BF16),
            pltpu.VMEM((fine, rows, channels // fine), F32),
            pltpu.SemaphoreType.DMA((2 * fine,)),
        ],
        input_output_aliases={3: 0},
        compiler_params=params(),
        name="end",
    )(last, skip_grad, projected.transpose(1, 0, 2), stacked)
    return mixed, grad_projected.transpose(1, 0, 2), grad_filter


def solution(mesh):
    in_specs = (
        P("seq", None, "chan"),
        P("chan"),
        P("chan", None),
        P("seq", "chan"),
        P("seq", "chan"),
    )
    out_specs = (P("seq", "chan"), P("seq", None, "chan"), P("seq", "chan"))
    return jax.shard_map(local, mesh=mesh, in_specs=in_specs, out_specs=out_specs, check_vma=False)
```
